256 devices in a mesh: tok: 16 (over z_lo, y, core), head: 16 (over x, z_hi).
Axes of the slice: x: 4, y: 4, z: 8 (z_hi: 4, z_lo: 2; z = z_hi * 2 + z_lo), core: 2. Of those that a mesh axis runs over, the one named last changes fastest.
Arguments:
- tokens: bfloat16 [8192, 4096], P('tok', 'head'), may hold values from -32 to 32
- w_query: bfloat16 [4096, 4096], P(None, 'head'), may hold values from -0.09375 to 0.09375
- w_key: bfloat16 [4096, 4096], P(None, 'head'), may hold values from -0.09375 to 0.09375
- w_value: bfloat16 [4096, 4096], P(None, 'head'), may hold values from -0.09375 to 0.09375
- w_out: bfloat16 [4096, 4096], P('head'), may hold values from -0.09375 to 0.09375
- fast_gate: float32 [32, 128, 256], P('head'), may hold values from -0.5 to 0.5
- fast_up: float32 [32, 128, 256], P('head'), may hold values from -0.5 to 0.5
- fast_down: float32 [32, 256, 128], P('head'), may hold values from -0.375 to 0.375
- token_rate: float32 [8192, 32], P('tok', 'head'), may hold values from 0.05 to 1
- head_step: float32 [32], P('head'), may hold values from 0.2 to 1
Outputs:
- mixed: bfloat16 [8192, 4096], P(('tok', 'head'))
The draws below stay inside these ranges and needn't reach their ends.
All inputs are finite; a program needn't handle non-finite values.
Results may differ from the reference program's by a relative error of at most 0.022.
Values may be sent and summed in bfloat16 or wider, within the bound.
A program may use at most 64 MiB of HBM per device.

```python
import math
import jax
import jax.numpy as jnp
from jax import lax

HEADS = 32
HEAD_DIM = 128
FAST_HID = 256
WINDOW = 512
TOK_DEV = 512
D = 4096
TOKENS = 8192


def draw_tokens(key, part):
    first_key = jax.random.fold_in(key, 11)
    base = jnp.clip(jax.random.normal(first_key, (TOKENS, D), jnp.float32), -4.0, 4.0)
    return base.astype(jnp.bfloat16)


def level_of(own_key, shape, pieces, least, largest):
    def one(position, shards_of):
        draws = jax.random.uniform(jax.random.fold_in(jax.random.fold_in(own_key, 6), position), (shards_of,), jnp.float32, least / len(pieces), largest / len(pieces))
        return jnp.repeat(jnp.exp(draws), shape[position] // shards_of).reshape((-1,) + (1,) * (len(shape) - position - 1))

    level = one(*pieces[0])
    for cut in pieces[1:]:
        level = level * one(*cut)
    return level


def bell_draw(own_key, extent, width, most, cuts=(), kind=jnp.bfloat16):
    values = jax.random.normal(own_key, extent, jnp.float32) * width
    if len(cuts) > 0:
        values = level_of(own_key, extent, cuts, -0.22, 0.18) * values
    return jnp.clip(values, min=-most, max=most).astype(kind)


def setup_inputs(seed: int = 0) -> dict:
    arg_keys = jax.random.split(jax.random.key(seed), 11)
    return {
        "tokens": draw_tokens(jax.random.fold_in(arg_keys[10], 71), 0),
        "w_query": bell_draw(arg_keys[1], (D, D), D ** -0.5, 0.09375, ((1, 16),)),
        "w_key": bell_draw(arg_keys[2], (D, D), D ** -0.5, 0.09375, ((1, 16),)),
        "w_value": bell_draw(arg_keys[3], (D, D), D ** -0.5, 0.09375, ((1, 16),)),
        "w_out": bell_draw(arg_keys[4], (D, D), D ** -0.5, 0.09375, ((0, 16),)),
        "fast_gate": bell_draw(arg_keys[5], (HEADS, HEAD_DIM, FAST_HID), HEAD_DIM ** -0.5, 0.5, ((0, 16),), jnp.float32),
        "fast_up": bell_draw(arg_keys[6], (HEADS, HEAD_DIM, FAST_HID), HEAD_DIM ** -0.5, 0.5, ((0, 16),), jnp.float32),
        "fast_down": bell_draw(arg_keys[7], (HEADS, FAST_HID, HEAD_DIM), FAST_HID ** -0.5, 0.375, ((0, 16),), jnp.float32),
        "token_rate": jnp.clip(jnp.exp(math.log(1.0) - 2.9957323 * jax.random.uniform(arg_keys[8], (TOKENS, HEADS), jnp.float32) ** level_of(arg_keys[8], (TOKENS, HEADS), ((0, 16), (1, 16)), -0.2, 0.2)), 0.05, 1.0),
        "head_step": jnp.clip(jnp.exp(math.log(1.0) - 1.609438 * jax.random.uniform(arg_keys[9], (HEADS,), jnp.float32) ** level_of(arg_keys[9], (HEADS,), ((0, 16),), -0.2, 0.2)), 0.2, 1.0),
    }


def rms(values):
    return values * lax.rsqrt(lax.optimization_barrier(jnp.mean(values * values, axis=-1, keepdims=True)) + 1e-06)

def matmul(left, right):
    return jnp.dot(left, right, precision=lax.Precision.HIGHEST)

def fast_apply(inputs, gate, upper, down):
    gate_pre = matmul(inputs, gate)
    return matmul(jax.nn.silu(gate_pre) * matmul(inputs, upper), down)

def renew(matrix, grad, step, fan_in):
    mean_sq = jnp.mean(grad * grad)
    return matrix - step * grad * lax.rsqrt(mean_sq + 1e-06) * fan_in ** (-0.5)

def one_head(items):
    query_h, key_h, value_h, rate_h, gate, upper, down, step = items
    knorm = rms(key_h.astype(jnp.float32))
    qnorm = rms(query_h.astype(jnp.float32))
    target = -rate_h[:, None] * value_h.astype(jnp.float32)
    gate_pre = matmul(knorm, gate)
    up_pre = matmul(knorm, upper)
    sigma = jax.nn.sigmoid(gate_pre)
    active = gate_pre * sigma
    hidden = active * up_pre
    grad_down = matmul(hidden.T, target)
    back = matmul(target, down.T)
    grad_up = matmul(knorm.T, back * active)
    grad_gate = matmul(knorm.T, back * up_pre * sigma * (1.0 + gate_pre * (1.0 - sigma)))
    new_gate = renew(gate, grad_gate, step, HEAD_DIM)
    new_up = renew(upper, grad_up, step, HEAD_DIM)
    new_down = renew(down, grad_down, step, FAST_HID)
    return fast_apply(qnorm, new_gate, new_up, new_down)

def reference(tokens, w_query, w_key, w_value, w_out, fast_gate, fast_up, fast_down, token_rate, head_step):
    shape = (TOKENS, HEADS, HEAD_DIM)
    query = jnp.dot(tokens, w_query, preferred_element_type=jnp.float32).astype(jnp.bfloat16).reshape(shape)
    key = jnp.dot(tokens, w_key, preferred_element_type=jnp.float32).astype(jnp.bfloat16).reshape(shape)
    value = jnp.dot(tokens, w_value, preferred_element_type=jnp.float32).astype(jnp.bfloat16).reshape(shape)
    padding = jnp.zeros((WINDOW, HEADS, HEAD_DIM), jnp.bfloat16)
    key_pad = jnp.concatenate([padding, key], axis=0)
    value_pad = jnp.concatenate([padding, value], axis=0)

    def block(index):
        first = index * TOK_DEV
        query_b = lax.dynamic_slice_in_dim(query, first, TOK_DEV, 0).astype(jnp.float32)
        key_b = lax.dynamic_slice_in_dim(key_pad, first, TOK_DEV + WINDOW, 0).astype(jnp.float32)
        value_b = lax.dynamic_slice_in_dim(value_pad, first, TOK_DEV + WINDOW, 0).astype(jnp.float32)
        query_pos = first + jnp.arange(TOK_DEV, dtype=jnp.int32)
        key_pos = first - WINDOW + jnp.arange(TOK_DEV + WINDOW, dtype=jnp.int32)
        allowed = (key_pos[None, :] >= 0) & (key_pos[None, :] <= query_pos[:, None]) & (key_pos[None, :] > query_pos[:, None] - WINDOW)
        scores = jnp.einsum('qhd,khd->hqk', query_b, key_b) * HEAD_DIM ** (-0.5)
        scores = jnp.where(allowed[None], scores, jnp.float32(-1e+30))
        top = lax.optimization_barrier(jnp.max(scores, axis=-1, keepdims=True))
        expo = jnp.exp(scores - top)
        weights = (expo / lax.optimization_barrier(jnp.sum(expo, axis=-1, keepdims=True))).astype(jnp.bfloat16)
        return jnp.einsum('hqk,khd->qhd', weights.astype(jnp.float32), value_b)
    attended = lax.map(block, jnp.arange(TOKENS // TOK_DEV, dtype=jnp.int32)).reshape(shape)
    items = (jnp.transpose(query, (1, 0, 2)), jnp.transpose(key, (1, 0, 2)), jnp.transpose(value, (1, 0, 2)), token_rate.T, fast_gate, fast_up, fast_down, head_step)
    fast_out = jnp.transpose(lax.map(one_head, items), (1, 0, 2))
    combined = (attended + fast_out).astype(jnp.bfloat16).reshape(TOKENS, D)
    return jnp.dot(combined, w_out, preferred_element_type=jnp.float32).astype(jnp.bfloat16)
```

```python
import functools
import heapq

import jax
import jax.numpy as jnp
from jax import lax
from jax.experimental import pallas as pl
from jax.experimental.pallas import tpu as pltpu
from jax.sharding import PartitionSpec as P

MESH = pl.DeviceIdType.MESH
WINDOW = 512
SIDE = 4
F32 = jnp.float32
BF16 = jnp.bfloat16
MIRRORS = ((1, 1), (-1, 1), (1, -1), (-1, -1))


def tree_of(sx, sz):
    come = {(0, sz % 4): ("z", sz), (0, -sz % 4): ("z", -sz)}
    for b in (0, 1, 3):
        come[(sx % 4, b)] = ("x", sx)
        come[(-sx % 4, b)] = ("x", -sx)
        come[(2, b)] = ("x", sx)
    come[(0, 2)] = ("z", sz)
    come[(-sx % 4, 2)] = ("x", -sx)
    come[(sx % 4, 2)] = ("z", -sz)
    come[(2, 2)] = ("z", sz)
    return come


def from_of(spot, way):
    axis, sign = way
    return ((spot[0] - sign) % 4, spot[1]) if axis == "x" else (spot[0], (spot[1] - sign) % 4)


def below_of(come):
    below = {}
    for spot, way in come.items():
        below.setdefault(from_of(spot, way), []).append(spot)
    return below


def height(below, spot):
    return max([1 + height(below, s) for s in below.get(spot, [])], default=0)


def plan(trees, size):
    rate = {"x": 46.8e3, "z": 23.4e3}
    late = {"x": 1.8, "z": 2.6}
    belows = [below_of(t) for t in trees]
    free = {(a, s): 0.0 for a in "xz" for s in (1, -1)}
    heap, count, order = [], 0, []

    def send(when, piece, spot):
        nonlocal count
        for to in sorted(belows[piece].get(spot, []), key=lambda s: -height(belows[piece], s)):
            way = trees[piece][to]
            begin = max(when, free[way])
            free[way] = begin + size / rate[way[0]]
            count += 1
            heapq.heappush(heap, (free[way] + late[way[0]], count, piece, to))

    for piece in range(len(trees)):
        send(0.0, piece, (0, 0))
    while heap:
        when, _, piece, spot = heapq.heappop(heap)
        order.append((piece, spot))
        send(when, piece, spot)
    return order


def slot(spot):
    return spot[0] * SIDE + spot[1]


def dot(a, b, dims=((1,), (0,))):
    return lax.dot_general(a, b, (dims, ((), ())), preferred_element_type=F32)


def unit(u):
    return u * lax.rsqrt(jnp.mean(u * u, axis=-1, keepdims=True) + 1e-06)


def kernel(
    tok_n, tokens, w_query, w_key, w_value, w_out, gate, upper, down, rate, step,
    out,
    blocks, w_in, w_o, acc, q, kv, g_w, u_w, d_w, kn_s, tg_s, hid_s, dup_s, dgate_s,
    grad, grad_in, grad_sum, att, comb, part, come_in, go_out,
    load_sem, ag_send, ag_recv, halo_send, halo_recv, ar_send, ar_recv, rs_send, rs_recv,
):
    rows = tokens.shape[0]
    width = tokens.shape[1]
    heads, head_size, hidden = g_w.shape
    t = lax.axis_index("tok")
    h = lax.axis_index("head")
    x, z = h // SIDE, lax.rem(h, SIDE)

    def at(way):
        axis, sign = way
        if axis == "x":
            return (t, lax.rem(x + (SIDE + sign), SIDE) * SIDE + z)
        return (t, x * SIDE + lax.rem(z + (SIDE + sign), SIDE))

    def owner(spot):
        a, b = spot
        return lax.rem(x + (SIDE - a), SIDE) * SIDE + lax.rem(z + (SIDE - b), SIDE)

    def tok_at(k):
        return (lax.rem(t + k, tok_n), h)

    loads = [pltpu.make_async_copy(tokens, blocks.at[0], load_sem.at[0])]
    for j, w in enumerate((w_query, w_key, w_value)):
        loads.append(pltpu.make_async_copy(w, w_in.at[j], load_sem.at[1 + j]))
    loads.append(pltpu.make_async_copy(gate, g_w, load_sem.at[4]))
    loads.append(pltpu.make_async_copy(upper, u_w, load_sem.at[5]))
    loads.append(pltpu.make_async_copy(down, d_w, load_sem.at[6]))
    loads.append(pltpu.make_async_copy(w_out, w_o, load_sem.at[7]))
    for c in loads:
        c.start()

    barrier = pltpu.get_barrier_semaphore()
    ways = [("x", 1), ("x", -1), ("z", 1), ("z", -1)]
    for way in ways:
        pl.semaphore_signal(barrier, inc=1, device_id=at(way), device_id_type=MESH)
    for k in range(1, tok_n):
        pl.semaphore_signal(barrier, inc=1, device_id=tok_at(k), device_id_type=MESH)
    pl.semaphore_wait(barrier, len(ways) + tok_n - 1)

    trees = [tree_of(*m) for m in MIRRORS]
    belows = [below_of(tr) for tr in trees]
    piece_rows = rows // len(trees)
    order = plan(trees, piece_rows * width * 2)

    def ag_copy(p, to):
        frm = from_of(to, trees[p][to])
        span = pl.ds(p * piece_rows, piece_rows)
        src = tokens.at[span] if frm == (0, 0) else blocks.at[slot(frm), span]
        k = p * 16 + slot(to)
        return pltpu.make_async_remote_copy(
            src_ref=src, dst_ref=blocks.at[slot(to), span], send_sem=ag_send.at[k], recv_sem=ag_recv.at[k],
            device_id=at(trees[p][to]), device_id_type=MESH,
        )

    def ag_forward(p, spot):
        for to in sorted(belows[p].get(spot, []), key=lambda s: -height(belows[p], s)):
            ag_copy(p, to).start()

    for p in range(len(trees)):
        ag_forward(p, (0, 0))

    def project(spot, first):
        base = pl.multiple_of(owner(spot) * width, width)

        def one(j, carry):
            prod = dot(blocks[slot(spot)], w_in[j, pl.ds(base, width)])
            acc[j] = prod if first else acc[j] + prod
            return carry

        lax.fori_loop(0, 3, one, 0)

    for c in loads[:4]:
        c.wait()
    project((0, 0), True)
    missing = {}
    for p, spot in order:
        ag_copy(p, spot).wait_recv()
        ag_forward(p, spot)
        missing[spot] = missing.get(spot, len(trees)) - 1
        if missing[spot] == 0:
            project(spot, False)

    for i in range(heads):
        cols = slice(i * head_size, (i + 1) * head_size)
        kv[i, pl.ds(WINDOW, rows)] = acc[1, :, cols].astype(BF16)
        kv[heads + i, pl.ds(WINDOW, rows)] = acc[2, :, cols].astype(BF16)
    halo = []
    for i in range(2 * heads):
        halo.append(pltpu.make_async_remote_copy(
            src_ref=kv.at[i, pl.ds(rows, WINDOW)], dst_ref=kv.at[i, pl.ds(0, WINDOW)],
            send_sem=halo_send.at[i], recv_sem=halo_recv.at[i], device_id=tok_at(1), device_id_type=MESH,
        ))
        halo[-1].start()
    for i in range(heads):
        q[i] = acc[0, :, i * head_size:(i + 1) * head_size].astype(BF16)

    for c in loads[4:7]:
        c.wait()
    chunk = 128

    def grads(i, carry):
        gw = g_w[i].astype(BF16)
        uw = u_w[i].astype(BF16)
        dw = d_w[i].astype(BF16)

        def some(r, inner):
            span = pl.ds(pl.multiple_of(r * chunk, chunk), chunk)
            here = pl.ds(pl.multiple_of(r * chunk, chunk) + WINDOW, chunk)
            kn = unit(kv[i, here].astype(F32)).astype(BF16)
            each = rate[span]
            lane = lax.broadcasted_iota(jnp.int32, each.shape, 1)
            mine = jnp.sum(jnp.where(lane == i, each, 0.0), axis=1, keepdims=True)
            tg = (-mine * kv[heads + i, here].astype(F32)).astype(BF16)
            gate_pre = dot(kn, gw)
            up_pre = dot(kn, uw)
            back = dot(tg, dw, ((1,), (1,)))
            sigma = jax.nn.sigmoid(gate_pre)
            active = gate_pre * sigma
            kn_s[span] = kn
            tg_s[span] = tg
            hid_s[span] = (active * up_pre).astype(BF16)
            dup_s[span] = (back * active).astype(BF16)
            dgate_s[span] = (back * up_pre * sigma * (1.0 + gate_pre * (1.0 - sigma))).astype(BF16)
            return inner

        lax.fori_loop(0, rows // chunk, some, 0)
        base = pl.multiple_of(i * (3 * head_size), head_size)
        kn_all = kn_s[...]
        grad[pl.ds(base, head_size)] = dot(kn_all, dgate_s[...], ((0,), (0,))).astype(BF16)
        grad[pl.ds(base + head_size, head_size)] = dot(kn_all, dup_s[...], ((0,), (0,))).astype(BF16)
        grad[pl.ds(base + 2 * head_size, head_size)] = dot(tg_s[...], hid_s[...], ((0,), (0,))).astype(BF16)
        return carry

    lax.fori_loop(0, heads, grads, 0)

    slice_rows = grad.shape[0] // tok_n
    scatter = []
    for k in range(1, tok_n):
        to = lax.rem(t + k, tok_n)
        scatter.append(pltpu.make_async_remote_copy(
            src_ref=grad.at[pl.ds(pl.multiple_of(to * slice_rows, slice_rows), slice_rows)], dst_ref=grad_in.at[k],
            send_sem=ar_send.at[k], recv_sem=ar_recv.at[k], device_id=(to, h), device_id_type=MESH,
        ))
        scatter[-1].start()

    def attend(i):
        keys_n = WINDOW + chunk

        def some(b, carry):
            first = pl.multiple_of(b * chunk, chunk)
            keys = kv[i, pl.ds(first, keys_n)]
            scores = dot(q[i, pl.ds(first, chunk)], keys, ((1,), (1,))) * head_size ** (-0.5)
            r = lax.broadcasted_iota(jnp.int32, scores.shape, 0)
            c = lax.broadcasted_iota(jnp.int32, scores.shape, 1)
            allowed = (c > r) & (c <= r + WINDOW) & (c >= WINDOW - first - t * rows)
            scores = jnp.where(allowed, scores, -1e30)
            top = jnp.max(scores, axis=-1, keepdims=True)
            expo = jnp.exp(scores - top)
            weights = (expo * (1.0 / jnp.sum(expo, axis=-1, keepdims=True))).astype(BF16)
            att[i, pl.ds(first, chunk)] = dot(weights, kv[heads + i, pl.ds(first, keys_n)])
            return carry

        lax.fori_loop(0, rows // chunk, some, 0)

    for c in halo:
        c.wait_recv()
    attend(0)

    mine = pl.ds(pl.multiple_of(t * slice_rows, slice_rows), slice_rows)
    total = grad[mine].astype(F32)
    for k, c in enumerate(scatter, 1):
        c.wait_recv()
        total = total + grad_in[k].astype(F32)
    grad_sum[mine] = total.astype(BF16)
    share = []
    for k in range(1, tok_n):
        share.append(pltpu.make_async_remote_copy(
            src_ref=grad_sum.at[mine], dst_ref=grad_sum.at[mine],
            send_sem=ar_send.at[tok_n + k], recv_sem=ar_recv.at[tok_n + k], device_id=tok_at(k), device_id_type=MESH,
        ))
        share[-1].start()
    for i in range(1, heads):
        attend(i)
    for c in share:
        c.wait_recv()

    def apply(i, carry):
        base = pl.multiple_of(i * (3 * head_size), head_size)

        def renew(j, matrix, fan_in):
            g = grad_sum[pl.ds(base + j * head_size, head_size)].astype(F32)
            mean_sq = jnp.sum(jnp.sum(g * g, axis=1, keepdims=True), axis=0, keepdims=True) / (head_size * hidden)
            return (matrix - (step[i] * fan_in ** (-0.5)) * g * lax.rsqrt(mean_sq + 1e-06)).astype(BF16)

        gw = renew(0, g_w[i], head_size)
        uw = renew(1, u_w[i], head_size)
        dw = renew(2, d_w[i].T, hidden)

        def some(r, inner):
            span = pl.ds(pl.multiple_of(r * chunk, chunk), chunk)
            qn = unit(q[i, span].astype(F32)).astype(BF16)
            gate_pre = dot(qn, gw)
            hid = (gate_pre * jax.nn.sigmoid(gate_pre) * dot(qn, uw)).astype(BF16)
            fast = dot(hid, dw, ((1,), (1,)))
            comb[span, pl.ds(pl.multiple_of(i * head_size, head_size), head_size)] = (att[i, span] + fast).astype(BF16)
            return inner

        lax.fori_loop(0, rows // chunk, some, 0)
        return carry

    lax.fori_loop(0, heads, apply, 0)

    loads[7].wait()
    out_rows = out.shape[0]
    piece_cols = out.shape[1] // len(trees)

    def rs_copy(p, spot):
        axis, sign = trees[p][spot]
        k = p * 16 + slot(spot)
        return pltpu.make_async_remote_copy(
            src_ref=go_out.at[k], dst_ref=come_in.at[k], send_sem=rs_send.at[k], recv_sem=rs_recv.at[k],
            device_id=at((axis, -sign)), device_id_type=MESH,
        )

    def gathered(p, spot):
        own = part[p, pl.ds(pl.multiple_of(owner(spot) * out_rows, out_rows), out_rows)]
        for child in belows[p].get(spot, []):
            rs_copy(p, child).wait_recv()
            own = own + come_in[p * 16 + slot(child)].astype(F32)
        return own.astype(BF16)

    ready = set()
    for p, spot in order[::-1]:
        if p not in ready:
            ready.add(p)

            def cols(j, carry, p=p):
                lanes = pl.ds(pl.multiple_of(j * 256, 256), 256)
                wide = pl.ds(pl.multiple_of(p * piece_cols + j * 256, 256), 256)
                part[p, :, lanes] = dot(comb[...], w_o[:, wide])
                return carry

            lax.fori_loop(0, piece_cols // 256, cols, 0)
        go_out[p * 16 + slot(spot)] = gathered(p, spot)
        rs_copy(p, spot).start()
    for p in range(len(trees)):
        out[:, p * piece_cols:(p + 1) * piece_cols] = gathered(p, (0, 0))

    for p, spot in order:
        ag_copy(p, spot).wait_send()
        rs_copy(p, spot).wait_send()
    for c in halo + scatter + share:
        c.wait_send()


def shards(
    tok_n, head_n, tokens, w_query, w_key, w_value, w_out, fast_gate, fast_up, fast_down, token_rate, head_step
):
    rows, width = tokens.shape
    depth, local_width = w_query.shape
    d_model = w_out.shape[1]
    heads, head_size, hidden = fast_gate.shape
    pieces = len(MIRRORS)
    any_space = pl.BlockSpec(memory_space=pl.ANY)
    vmem = pl.BlockSpec(memory_space=pltpu.VMEM)
    smem = pl.BlockSpec(memory_space=pltpu.SMEM)
    dma = pltpu.SemaphoreType.DMA
    return pl.pallas_call(
        functools.partial(kernel, tok_n),
        out_shape=jax.ShapeDtypeStruct((rows // head_n, d_model), BF16),
        in_specs=[any_space] * 8 + [vmem, smem],
        out_specs=vmem,
        scratch_shapes=[
            pltpu.VMEM((head_n, rows, width), BF16),
            pltpu.VMEM((3, depth, local_width), BF16),
            pltpu.VMEM((local_width, d_model), BF16),
            pltpu.VMEM((3, rows, local_width), F32),
            pltpu.VMEM((heads, rows, head_size), BF16),
            pltpu.VMEM((2 * heads, WINDOW + rows, head_size), BF16),
            pltpu.VMEM((heads, head_size, hidden), F32),
            pltpu.VMEM((heads, head_size, hidden), F32),
            pltpu.VMEM((heads, hidden, head_size), F32),
            pltpu.VMEM((rows, head_size), BF16),
            pltpu.VMEM((rows, head_size), BF16),
            pltpu.VMEM((rows, hidden), BF16),
            pltpu.VMEM((rows, hidden), BF16),
            pltpu.VMEM((rows, hidden), BF16),
            pltpu.VMEM((heads * 3 * head_size, hidden), BF16),
            pltpu.VMEM((tok_n, heads * 3 * head_size // tok_n, hidden), BF16),
            pltpu.VMEM((heads * 3 * head_size, hidden), BF16),
            pltpu.VMEM((heads, rows, head_size), F32),
            pltpu.VMEM((rows, local_width), BF16),
            pltpu.VMEM((pieces, rows, d_model // pieces), F32),
            pltpu.VMEM((pieces * 16, rows // head_n, d_model // pieces), BF16),
            pltpu.VMEM((pieces * 16, rows // head_n, d_model // pieces), BF16),
            dma((8,)), dma((pieces * 16,)), dma((pieces * 16,)), dma((2 * heads,)), dma((2 * heads,)),
            dma((2 * tok_n,)), dma((2 * tok_n,)), dma((pieces * 16,)), dma((pieces * 16,)),
        ],
        compiler_params=pltpu.CompilerParams(
            collective_id=0, has_side_effects=True, vmem_limit_bytes=60 * 2**20
        ),
    )(tokens, w_query, w_key, w_value, w_out, fast_gate, fast_up, fast_down, token_rate, head_step)


def solution(mesh):
    placed = (
        P("tok", "head"),
        P(None, "head"),
        P(None, "head"),
        P(None, "head"),
        P("head", None),
        P("head", None, None),
        P("head", None, None),
        P("head", None, None),
        P("tok", "head"),
        P("head"),
    )
    return jax.shard_map(
        functools.partial(shards, mesh.shape["tok"], mesh.shape["head"]),
        mesh=mesh, in_specs=placed, out_specs=P(("tok", "head"), None), check_vma=False,
    )
```

```python
import functools
import heapq

import jax
import jax.numpy as jnp
from jax import lax
from jax.experimental import pallas as pl
from jax.experimental.pallas import tpu as pltpu
from jax.sharding import PartitionSpec as P

MESH = pl.DeviceIdType.MESH
WINDOW = 512
SIDE = 4
F32 = jnp.float32
BF16 = jnp.bfloat16
MIRRORS = ((1, 1), (-1, 1), (1, -1), (-1, -1))


def tree_of(sx, sz):
    come = {(0, sz % 4): ("z", sz), (0, -sz % 4): ("z", -sz)}
    for b in (0, 1, 3):
        come[(sx % 4, b)] = ("x", sx)
        come[(-sx % 4, b)] = ("x", -sx)
        come[(2, b)] = ("x", sx)
    come[(0, 2)] = ("z", sz)
    come[(-sx % 4, 2)] = ("x", -sx)
    come[(sx % 4, 2)] = ("z", -sz)
    come[(2, 2)] = ("z", sz)
    return come


def from_of(spot, way):
    axis, sign = way
    return ((spot[0] - sign) % 4, spot[1]) if axis == "x" else (spot[0], (spot[1] - sign) % 4)


def below_of(come):
    below = {}
    for spot, way in come.items():
        below.setdefault(from_of(spot, way), []).append(spot)
    return below


def height(below, spot):
    return max([1 + height(below, s) for s in below.get(spot, [])], default=0)


def plan(trees, size):
    rate = {"x": 46.8e3, "z": 23.4e3}
    late = {"x": 1.8, "z": 2.6}
    belows = [below_of(t) for t in trees]
    free = {(a, s): 0.0 for a in "xz" for s in (1, -1)}
    heap, count, order = [], 0, []

    def send(when, piece, spot):
        nonlocal count
        for to in sorted(belows[piece].get(spot, []), key=lambda s: -height(belows[piece], s)):
            way = trees[piece][to]
            begin = max(when, free[way])
            free[way] = begin + size / rate[way[0]]
            count += 1
            heapq.heappush(heap, (free[way] + late[way[0]], count, piece, to))

    for piece in range(len(trees)):
        send(0.0, piece, (0, 0))
    while heap:
        when, _, piece, spot = heapq.heappop(heap)
        order.append((piece, spot))
        send(when, piece, spot)
    return order


def slot(spot):
    return spot[0] * SIDE + spot[1]


def dot(a, b, dims=((1,), (0,))):
    return lax.dot_general(a, b, (dims, ((), ())), preferred_element_type=F32)


def unit(u):
    return u * lax.rsqrt(jnp.mean(u * u, axis=-1, keepdims=True) + 1e-06)


def kernel(
    tok_n, tokens, w_query, w_key, w_value, w_out, gate, upper, down, rate, step,
    out,
    blocks, w_in, w_o, acc, q, kv, g_w, u_w, d_w,
    grad, pair_in, half, chip_in, grad_sum, att, comb, part, come_in, go_out,
    load_sem, ag_send, ag_recv, halo_send, halo_recv, ar_send, ar_recv, rs_send, rs_recv,
):
    rows = tokens.shape[0]
    width = tokens.shape[1]
    heads, head_size, hidden = g_w.shape
    t = lax.axis_index("tok")
    h = lax.axis_index("head")
    x, z = h // SIDE, lax.rem(h, SIDE)

    def at(way):
        axis, sign = way
        if axis == "x":
            return (t, lax.rem(x + (SIDE + sign), SIDE) * SIDE + z)
        return (t, x * SIDE + lax.rem(z + (SIDE + sign), SIDE))

    def owner(spot):
        a, b = spot
        return lax.rem(x + (SIDE - a), SIDE) * SIDE + lax.rem(z + (SIDE - b), SIDE)

    def tok_at(k):
        return (lax.rem(t + k, tok_n), h)

    loads = [pltpu.make_async_copy(tokens, blocks.at[0], load_sem.at[0])]
    for j, w in enumerate((w_query, w_key, w_value)):
        loads.append(pltpu.make_async_copy(w, w_in.at[j], load_sem.at[1 + j]))
    loads.append(pltpu.make_async_copy(gate, g_w, load_sem.at[4]))
    loads.append(pltpu.make_async_copy(upper, u_w, load_sem.at[5]))
    loads.append(pltpu.make_async_copy(down, d_w, load_sem.at[6]))
    loads.append(pltpu.make_async_copy(w_out, w_o, load_sem.at[7]))
    for c in loads:
        c.start()

    barrier = pltpu.get_barrier_semaphore()
    ways = [("x", 1), ("x", -1), ("z", 1), ("z", -1)]
    for way in ways:
        pl.semaphore_signal(barrier, inc=1, device_id=at(way), device_id_type=MESH)
    near = [1, tok_n - 1] + list(range(2, tok_n, 2))
    for k in near:
        pl.semaphore_signal(barrier, inc=1, device_id=tok_at(k), device_id_type=MESH)
    pl.semaphore_wait(barrier, len(ways) + len(near))

    trees = [tree_of(*m) for m in MIRRORS]
    belows = [below_of(tr) for tr in trees]
    piece_rows = rows // len(trees)
    order = plan(trees, piece_rows * width * 2)

    def ag_copy(p, to):
        frm = from_of(to, trees[p][to])
        span = pl.ds(p * piece_rows, piece_rows)
        src = tokens.at[span] if frm == (0, 0) else blocks.at[slot(frm), span]
        k = p * 16 + slot(to)
        return pltpu.make_async_remote_copy(
            src_ref=src, dst_ref=blocks.at[slot(to), span], send_sem=ag_send.at[k], recv_sem=ag_recv.at[k],
            device_id=at(trees[p][to]), device_id_type=MESH,
        )

    def ag_forward(p, spot):
        for to in sorted(belows[p].get(spot, []), key=lambda s: -height(belows[p], s)):
            ag_copy(p, to).start()

    for p in range(len(trees)):
        ag_forward(p, (0, 0))

    def project(spot, first):
        base = pl.multiple_of(owner(spot) * width, width)

        def one(j, carry):
            prod = dot(blocks[slot(spot)], w_in[j, pl.ds(base, width)])
            acc[j] = prod if first else acc[j] + prod
            return carry

        lax.fori_loop(0, 3, one, 0)

    for c in loads[:4]:
        c.wait()
    project((0, 0), True)
    missing = {}
    for p, spot in order:
        ag_copy(p, spot).wait_recv()
        ag_forward(p, spot)
        missing[spot] = missing.get(spot, len(trees)) - 1
        if missing[spot] == 0:
            project(spot, False)

    for i in range(heads):
        cols = slice(i * head_size, (i + 1) * head_size)
        kv[i, pl.ds(WINDOW, rows)] = acc[1, :, cols].astype(BF16)
        kv[heads + i, pl.ds(WINDOW, rows)] = acc[2, :, cols].astype(BF16)
    halo = []
    for i in range(2 * heads):
        halo.append(pltpu.make_async_remote_copy(
            src_ref=kv.at[i, pl.ds(rows, WINDOW)], dst_ref=kv.at[i, pl.ds(0, WINDOW)],
            send_sem=halo_send.at[i], recv_sem=halo_recv.at[i], device_id=tok_at(1), device_id_type=MESH,
        ))
        halo[-1].start()

    for c in loads[4:7]:
        c.wait()
    core = lax.rem(t, 2)
    chip = t // 2
    chips = tok_n // 2
    other = (t + 1 - 2 * core, h)
    half_rows = head_size // 2
    own_half = pl.ds(pl.multiple_of(core * half_rows, half_rows), half_rows)
    other_half = pl.ds(pl.multiple_of((1 - core) * half_rows, half_rows), half_rows)
    cut_rows, cut_cols = 2 * half_rows // chips, 3 * hidden // 2

    def cut(s, base=0):
        return (
            pl.ds(pl.multiple_of(base + (s // 2) * cut_rows, cut_rows), cut_rows),
            pl.ds(pl.multiple_of(lax.rem(s, 2) * cut_cols, cut_cols), cut_cols),
        )

    def column(row):
        n = row.shape[1]
        wide = jnp.broadcast_to(row, (n, n))
        eye = lax.broadcasted_iota(jnp.int32, (n, n), 0) == lax.broadcasted_iota(jnp.int32, (n, n), 1)
        return jnp.sum(jnp.where(eye, wide, 0.0), axis=1, keepdims=True)

    def ar_copy(kind, i, src, dst, to):
        k = kind * heads + i
        return pltpu.make_async_remote_copy(
            src_ref=src, dst_ref=dst, send_sem=ar_send.at[k], recv_sem=ar_recv.at[k], device_id=to, device_id_type=MESH,
        )

    pair = [ar_copy(0, i, grad.at[i, other_half], pair_in.at[i], other) for i in range(heads)]
    here = pl.ds(WINDOW, rows)
    for i in range(heads):
        gw = g_w[i].astype(BF16)
        uw = u_w[i].astype(BF16)
        dw = d_w[i].astype(BF16)
        kn = unit(kv[i, here].astype(F32)).astype(BF16)
        each = jnp.concatenate([column(rate[i:i + 1, r:r + 128]) for r in range(0, rows, 128)], axis=0)
        tg = (-each * kv[heads + i, here].astype(F32)).astype(BF16)
        gate_pre = dot(kn, gw)
        up_pre = dot(kn, uw)
        back = dot(tg, dw, ((1,), (1,)))
        sigma = jax.nn.sigmoid(gate_pre)
        active = gate_pre * sigma
        hid = (active * up_pre).astype(BF16)
        d_up = (back * active).astype(BF16)
        d_gate = (back * up_pre * sigma * (1.0 + gate_pre * (1.0 - sigma))).astype(BF16)
        grad[i, :, 0:hidden] = dot(kn, d_gate, ((0,), (0,))).astype(BF16)
        grad[i, :, hidden:2 * hidden] = dot(kn, d_up, ((0,), (0,))).astype(BF16)
        grad[i, :, 2 * hidden:] = dot(tg, hid, ((0,), (0,))).astype(BF16)
        pair[i].start()
    for i in range(heads):
        q[i] = acc[0, :, i * head_size:(i + 1) * head_size].astype(BF16)

    cross = []
    for i in range(heads):
        pair[i].wait_recv()
        half[i] = (grad[i, own_half].astype(F32) + pair_in[i].astype(F32)).astype(BF16)
        for k in range(1, chips):
            to = lax.rem(chip + k, chips)
            cross.append(ar_copy(1 + k, i, half.at[(i,) + cut(to)], chip_in.at[i, k], (to * 2 + core, h)))
            cross[-1].start()
    back_to = []
    mine = cut(chip, core * half_rows)
    for i in range(heads):
        total = half[(i,) + cut(chip)].astype(F32)
        for k in range(1, chips):
            cross[i * (chips - 1) + k - 1].wait_recv()
            total = total + chip_in[i, k].astype(F32)
        grad_sum[(i,) + mine] = total.astype(BF16)
        for k in range(1, chips):
            to = lax.rem(chip + k, chips)
            spot = grad_sum.at[(i,) + mine]
            back_to.append(ar_copy(chips + k, i, spot, spot, (to * 2 + core, h)))
            back_to[-1].start()

    def attend(i):
        chunk = 128
        keys_n = WINDOW + chunk
        for b in range(rows // chunk):
            first = b * chunk
            keys = kv[i, first:first + keys_n]
            scores = dot(q[i, first:first + chunk], keys, ((1,), (1,))) * head_size ** (-0.5)
            r = lax.broadcasted_iota(jnp.int32, scores.shape, 0)
            c = lax.broadcasted_iota(jnp.int32, scores.shape, 1)
            allowed = (c > r) & (c <= r + WINDOW) & (c >= WINDOW - first - t * rows)
            scores = jnp.where(allowed, scores, -1e30)
            top = jnp.max(scores, axis=-1, keepdims=True)
            expo = jnp.exp(scores - top)
            weights = (expo * (1.0 / jnp.sum(expo, axis=-1, keepdims=True))).astype(BF16)
            att[i, first:first + chunk] = dot(weights, kv[heads + i, first:first + keys_n])

    for c in halo:
        c.wait_recv()
    for i in range(heads):
        attend(i)
    last = []
    for i in range(heads):
        for k in range(1, chips):
            back_to[i * (chips - 1) + k - 1].wait_recv()
        spot = grad_sum.at[i, own_half]
        last.append(ar_copy(2 * chips, i, spot, spot, other))
        last[-1].start()

    for i in range(heads):
        last[i].wait_recv()

        def renew(j, matrix, fan_in):
            g = grad_sum[i, :, j * hidden:(j + 1) * hidden].astype(F32)
            mean_sq = jnp.sum(jnp.sum(g * g, axis=1, keepdims=True), axis=0, keepdims=True) / (head_size * hidden)
            return (matrix - (step[i] * fan_in ** (-0.5)) * g * lax.rsqrt(mean_sq + 1e-06)).astype(BF16)

        gw = renew(0, g_w[i], head_size)
        uw = renew(1, u_w[i], head_size)
        dw = renew(2, d_w[i].T, hidden)
        qn = unit(q[i].astype(F32)).astype(BF16)
        gate_pre = dot(qn, gw)
        hid = (gate_pre * jax.nn.sigmoid(gate_pre) * dot(qn, uw)).astype(BF16)
        fast = dot(hid, dw, ((1,), (1,)))
        comb[:, i * head_size:(i + 1) * head_size] = (att[i] + fast).astype(BF16)

    loads[7].wait()
    out_rows = out.shape[0]
    piece_cols = out.shape[1] // len(trees)

    def rs_copy(p, spot):
        axis, sign = trees[p][spot]
        k = p * 16 + slot(spot)
        return pltpu.make_async_remote_copy(
            src_ref=go_out.at[k], dst_ref=come_in.at[k], send_sem=rs_send.at[k], recv_sem=rs_recv.at[k],
            device_id=at((axis, -sign)), device_id_type=MESH,
        )

    def gathered(p, spot):
        own = part[p, pl.ds(pl.multiple_of(owner(spot) * out_rows, out_rows), out_rows)]
        for child in belows[p].get(spot, []):
            rs_copy(p, child).wait_recv()
            own = own + come_in[p * 16 + slot(child)].astype(F32)
        return own.astype(BF16)

    ready = set()
    for p, spot in order[::-1]:
        if p not in ready:
            ready.add(p)

            def cols(j, carry, p=p):
                lanes = pl.ds(pl.multiple_of(j * 256, 256), 256)
                wide = pl.ds(pl.multiple_of(p * piece_cols + j * 256, 256), 256)
                part[p, :, lanes] = dot(comb[...], w_o[:, wide])
                return carry

            lax.fori_loop(0, piece_cols // 256, cols, 0)
        go_out[p * 16 + slot(spot)] = gathered(p, spot)
        rs_copy(p, spot).start()
    for p in range(len(trees)):
        out[:, p * piece_cols:(p + 1) * piece_cols] = gathered(p, (0, 0))

    for p, spot in order:
        ag_copy(p, spot).wait_send()
        rs_copy(p, spot).wait_send()
    for c in halo + pair + cross + back_to + last:
        c.wait_send()


def shards(
    tok_n, head_n, tokens, w_query, w_key, w_value, w_out, fast_gate, fast_up, fast_down, token_rate, head_step
):
    rows, width = tokens.shape
    depth, local_width = w_query.shape
    d_model = w_out.shape[1]
    heads, head_size, hidden = fast_gate.shape
    pieces = len(MIRRORS)
    any_space = pl.BlockSpec(memory_space=pl.ANY)
    vmem = pl.BlockSpec(memory_space=pltpu.VMEM)
    smem = pl.BlockSpec(memory_space=pltpu.SMEM)
    dma = pltpu.SemaphoreType.DMA
    return pl.pallas_call(
        functools.partial(kernel, tok_n),
        out_shape=jax.ShapeDtypeStruct((rows // head_n, d_model), BF16),
        in_specs=[any_space] * 8 + [vmem, smem],
        out_specs=vmem,
        scratch_shapes=[
            pltpu.VMEM((head_n, rows, width), BF16),
            pltpu.VMEM((3, depth, local_width), BF16),
            pltpu.VMEM((local_width, d_model), BF16),
            pltpu.VMEM((3, rows, local_width), F32),
            pltpu.VMEM((heads, rows, head_size), BF16),
            pltpu.VMEM((2 * heads, WINDOW + rows, head_size), BF16),
            pltpu.VMEM((heads, head_size, hidden), F32),
            pltpu.VMEM((heads, head_size, hidden), F32),
            pltpu.VMEM((heads, hidden, head_size), F32),
            pltpu.VMEM((heads, head_size, 3 * hidden), BF16),
            pltpu.VMEM((heads, head_size // 2, 3 * hidden), BF16),
            pltpu.VMEM((heads, head_size // 2, 3 * hidden), BF16),
            pltpu.VMEM((heads, tok_n // 2, 2 * head_size // tok_n, 3 * hidden // 2), BF16),
            pltpu.VMEM((heads, head_size, 3 * hidden), BF16),
            pltpu.VMEM((heads, rows, head_size), F32),
            pltpu.VMEM((rows, local_width), BF16),
            pltpu.VMEM((pieces, rows, d_model // pieces), F32),
            pltpu.VMEM((pieces * 16, rows // head_n, d_model // pieces), BF16),
            pltpu.VMEM((pieces * 16, rows // head_n, d_model // pieces), BF16),
            dma((8,)), dma((pieces * 16,)), dma((pieces * 16,)), dma((2 * heads,)), dma((2 * heads,)),
            dma(((tok_n + 1) * heads,)), dma(((tok_n + 1) * heads,)), dma((pieces * 16,)), dma((pieces * 16,)),
        ],
        compiler_params=pltpu.CompilerParams(
            collective_id=0, has_side_effects=True, vmem_limit_bytes=60 * 2**20
        ),
    )(tokens, w_query, w_key, w_value, w_out, fast_gate, fast_up, fast_down, token_rate.T, head_step)


def solution(mesh):
    placed = (
        P("tok", "head"),
        P(None, "head"),
        P(None, "head"),
        P(None, "head"),
        P("head", None),
        P("head", None, None),
        P("head", None, None),
        P("head", None, None),
        P("tok", "head"),
        P("head"),
    )
    return jax.shard_map(
        functools.partial(shards, mesh.shape["tok"], mesh.shape["head"]),
        mesh=mesh, in_specs=placed, out_specs=P(("tok", "head"), None), check_vma=False,
    )
```

```python
import functools
import heapq

import jax
import jax.numpy as jnp
from jax import lax
from jax.experimental import pallas as pl
from jax.experimental.pallas import tpu as pltpu
from jax.sharding import PartitionSpec as P

MESH = pl.DeviceIdType.MESH
WINDOW = 512
SIDE = 4
RX, RZ, LX, LZ = 43.5e3, 21.7e3, 1.8, 3.5
AHEAD = 2.0
PART = 0.7
LAG = 24
F32 = jnp.float32
BF16 = jnp.bfloat16
MIRRORS = ((1, 1), (-1, 1), (1, -1), (-1, -1))


def tree_of(sx, sz):
    come = {(0, sz % 4): ("z", sz), (0, -sz % 4): ("z", -sz)}
    for b in (0, 1, 3):
        come[(sx % 4, b)] = ("x", sx)
        come[(-sx % 4, b)] = ("x", -sx)
        come[(2, b)] = ("x", sx)
    come[(0, 2)] = ("z", sz)
    come[(-sx % 4, 2)] = ("x", -sx)
    come[(sx % 4, 2)] = ("z", -sz)
    come[(2, 2)] = ("z", sz)
    return come


def from_of(spot, way):
    axis, sign = way
    return ((spot[0] - sign) % 4, spot[1]) if axis == "x" else (spot[0], (spot[1] - sign) % 4)


def below_of(come):
    below = {}
    for spot, way in come.items():
        below.setdefault(from_of(spot, way), []).append(spot)
    return below


def height(below, spot):
    return max([1 + height(below, s) for s in below.get(spot, [])], default=0)


def plan(trees, size):
    rate = {"x": RX, "z": RZ}
    late = {"x": LX, "z": LZ}
    belows = [below_of(t) for t in trees]
    queue = {(a, s): [] for a in "xz" for s in (1, -1)}
    free = dict.fromkeys(queue, 0.0)
    heap, count, done = [], 0, []

    def add(piece, spot):
        nonlocal count
        for to in belows[piece].get(spot, []):
            count += 1
            rank = -height(belows[piece], to)
            heapq.heappush(queue[trees[piece][to]], (rank, count, piece, to))

    def run(now):
        nonlocal count
        for way, waiting in queue.items():
            if waiting and free[way] <= now:
                _, _, piece, to = heapq.heappop(waiting)
                free[way] = now + size / rate[way[0]]
                count += 1
                heapq.heappush(heap, (free[way], count, None))
                count += 1
                heapq.heappush(heap, (free[way] + late[way[0]], count, (now, piece, to)))

    for piece in range(len(trees)):
        add(piece, (0, 0))
    run(0.0)
    while heap:
        now, _, got = heapq.heappop(heap)
        if got:
            done.append((got[0], now, got[1], got[2]))
            add(got[1], got[2])
        run(now)
    return done


def plan_back(trees, size, times):
    rate = {"x": RX, "z": RZ}
    late = {"x": LX, "z": LZ}
    belows = [below_of(t) for t in trees]
    rank = {(p, spot): -end for _, end, p, spot in times}
    left = {(p, spot): len(belows[p].get(spot, [])) + 1 for p, spot in rank}
    queue = {(a, s): [] for a in "xz" for s in (1, -1)}
    free = dict.fromkeys(queue, 0.0)
    heap = [(PART * (p + 1), p, (p, spot)) for p, spot in rank]
    heapq.heapify(heap)
    count, order = len(trees), []
    while heap:
        now, _, got = heapq.heappop(heap)
        if got and got[1] != (0, 0):
            left[got] -= 1
            if left[got] == 0:
                heapq.heappush(queue[trees[got[0]][got[1]]], (rank[got], got))
        if heap and heap[0][0] == now:
            continue
        for way, waiting in queue.items():
            if waiting and free[way] <= now:
                _, (p, spot) = heapq.heappop(waiting)
                free[way] = now + size / rate[way[0]]
                order.append((now, p, spot))
                count += 1
                heapq.heappush(heap, (free[way], count, None))
                count += 1
                heapq.heappush(heap, (free[way] + late[way[0]], count, (p, from_of(spot, trees[p][spot]))))
    return order


def slot(spot):
    return spot[0] * SIDE + spot[1]


def dot(a, b, dims=((1,), (0,))):
    return lax.dot_general(a, b, (dims, ((), ())), preferred_element_type=F32)


def unit(u):
    return u * lax.rsqrt(jnp.mean(u * u, axis=-1, keepdims=True) + 1e-06)


def kernel(
    tok_n, tokens, w_query, w_key, w_value, w_out, gate, upper, down, rate, step,
    out,
    blocks, w_in, w_o, acc, q, kv, g_w, u_w, d_w,
    grad, pair_in, half, chip_in, grad_sum, att, comb, part, come_in, go_out,
    load_sem, ag_send, ag_recv, halo_send, halo_recv, ar_send, ar_recv, rs_send, rs_recv,
):
    rows = tokens.shape[0]
    width = tokens.shape[1]
    heads, head_size, hidden = g_w.shape
    t = lax.axis_index("tok")
    h = lax.axis_index("head")
    x, z = h // SIDE, lax.rem(h, SIDE)

    def at_(way):
        axis, sign = way
        if axis == "x":
            return (t, lax.rem(x + (SIDE + sign), SIDE) * SIDE + z)
        return (t, x * SIDE + lax.rem(z + (SIDE + sign), SIDE))

    nbr = {(a, s): at_((a, s)) for a in "xz" for s in (1, -1)}

    def at(way):
        return nbr[way]

    def owner(spot):
        a, b = spot
        return lax.rem(x + (SIDE - a), SIDE) * SIDE + lax.rem(z + (SIDE - b), SIDE)

    def tok_at(k):
        return (lax.rem(t + k, tok_n), h)

    loads = [pltpu.make_async_copy(tokens, blocks.at[0], load_sem.at[0])]
    for j, w in enumerate((w_query, w_key, w_value)):
        loads.append(pltpu.make_async_copy(w, w_in.at[j], load_sem.at[1 + j]))
    loads.append(pltpu.make_async_copy(gate, g_w, load_sem.at[4]))
    loads.append(pltpu.make_async_copy(upper, u_w, load_sem.at[5]))
    loads.append(pltpu.make_async_copy(down, d_w, load_sem.at[6]))
    loads.append(pltpu.make_async_copy(w_out, w_o, load_sem.at[7]))
    for c in loads:
        c.start()

    barrier = pltpu.get_barrier_semaphore()
    ways = [("x", 1), ("x", -1), ("z", 1), ("z", -1)]
    for way in ways:
        pl.semaphore_signal(barrier, inc=1, device_id=at(way), device_id_type=MESH)
    near = [1, tok_n - 1] + list(range(2, tok_n, 2))
    for k in near:
        pl.semaphore_signal(barrier, inc=1, device_id=tok_at(k), device_id_type=MESH)
    pl.semaphore_wait(barrier, len(ways) + len(near))

    trees = [tree_of(*m) for m in MIRRORS]
    belows = [below_of(tr) for tr in trees]
    piece_rows = rows // len(trees)
    times = plan(trees, piece_rows * width * 2)
    order = [(p, spot) for _, _, p, spot in times]
    script = [(end, 0, p, spot) for _, end, p, spot in times]
    came = {(p, spot): end for _, end, p, spot in times}
    for begin, _, p, spot in times:
        frm = from_of(spot, trees[p][spot])
        script.append((max(begin - AHEAD, came.get((p, frm), -1.0)), 1, p, spot))
    script.sort(key=lambda e: e[:2])

    def ag_copy(p, to):
        frm = from_of(to, trees[p][to])
        span = pl.ds(p * piece_rows, piece_rows)
        src = tokens.at[span] if frm == (0, 0) else blocks.at[slot(frm), span]
        k = p * 16 + slot(to)
        return pltpu.make_async_remote_copy(
            src_ref=src, dst_ref=blocks.at[slot(to), span], send_sem=ag_send.at[k], recv_sem=ag_recv.at[k],
            device_id=at(trees[p][to]), device_id_type=MESH,
        )

    early = [e for e in script if e[1] == 1 and e[0] <= 0.0]
    script = [e for e in script if not (e[1] == 1 and e[0] <= 0.0)]
    for _, _, p, spot in early:
        ag_copy(p, spot).start()

    def project(spot, first):
        base = pl.multiple_of(owner(spot) * width, width)

        def one(j, carry):
            prod = dot(blocks[slot(spot)], w_in[j, pl.ds(base, width)])
            acc[j] = prod if first else acc[j] + prod
            return carry

        lax.fori_loop(0, 3, one, 0)

    for c in loads[:4]:
        c.wait()
    project((0, 0), True)
    missing = {}
    for _, sends, p, spot in script:
        if sends:
            ag_copy(p, spot).start()
            continue
        ag_copy(p, spot).wait_recv()
        missing[spot] = missing.get(spot, len(trees)) - 1
        if missing[spot] == 0:
            project(spot, False)

    for i in range(heads):
        cols = slice(i * head_size, (i + 1) * head_size)
        kv[i, pl.ds(WINDOW, rows)] = acc[1, :, cols].astype(BF16)
        kv[heads + i, pl.ds(WINDOW, rows)] = acc[2, :, cols].astype(BF16)
    halo = []
    for i in range(2 * heads):
        halo.append(pltpu.make_async_remote_copy(
            src_ref=kv.at[i, pl.ds(rows, WINDOW)], dst_ref=kv.at[i, pl.ds(0, WINDOW)],
            send_sem=halo_send.at[i], recv_sem=halo_recv.at[i], device_id=tok_at(1), device_id_type=MESH,
        ))
        halo[-1].start()

    for c in loads[4:7]:
        c.wait()
    core = lax.rem(t, 2)
    chip = t // 2
    chips = tok_n // 2
    other = (t + 1 - 2 * core, h)
    half_rows = head_size // 2
    own_half = pl.ds(pl.multiple_of(core * half_rows, half_rows), half_rows)
    other_half = pl.ds(pl.multiple_of((1 - core) * half_rows, half_rows), half_rows)
    cut_rows, cut_cols = 2 * half_rows // chips, 3 * hidden // 2

    def cut(s, base=0):
        return (
            pl.ds(pl.multiple_of(base + (s // 2) * cut_rows, cut_rows), cut_rows),
            pl.ds(pl.multiple_of(lax.rem(s, 2) * cut_cols, cut_cols), cut_cols),
        )

    def column(row):
        n = row.shape[1]
        wide = jnp.broadcast_to(row, (n, n))
        eye = lax.broadcasted_iota(jnp.int32, (n, n), 0) == lax.broadcasted_iota(jnp.int32, (n, n), 1)
        return jnp.sum(jnp.where(eye, wide, 0.0), axis=1, keepdims=True)

    def ar_copy(kind, i, src, dst, to):
        k = kind * heads + i
        return pltpu.make_async_remote_copy(
            src_ref=src, dst_ref=dst, send_sem=ar_send.at[k], recv_sem=ar_recv.at[k], device_id=to, device_id_type=MESH,
        )

    pair = [ar_copy(0, i, grad.at[i, other_half], pair_in.at[i], other) for i in range(heads)]
    here = pl.ds(WINDOW, rows)
    for i in range(heads):
        gw = g_w[i].astype(BF16)
        uw = u_w[i].astype(BF16)
        dw = d_w[i].astype(BF16)
        kn = unit(kv[i, here].astype(F32)).astype(BF16)
        each = jnp.concatenate([column(rate[i:i + 1, r:r + 128]) for r in range(0, rows, 128)], axis=0)
        tg = (-each * kv[heads + i, here].astype(F32)).astype(BF16)
        gate_pre = dot(kn, gw)
        up_pre = dot(kn, uw)
        back = dot(tg, dw, ((1,), (1,)))
        sigma = jax.nn.sigmoid(gate_pre)
        active = gate_pre * sigma
        hid = (active * up_pre).astype(BF16)
        d_up = (back * active).astype(BF16)
        d_gate = (back * up_pre * sigma * (1.0 + gate_pre * (1.0 - sigma))).astype(BF16)
        grad[i, :, 0:hidden] = dot(kn, d_gate, ((0,), (0,))).astype(BF16)
        grad[i, :, hidden:2 * hidden] = dot(kn, d_up, ((0,), (0,))).astype(BF16)
        grad[i, :, 2 * hidden:] = dot(tg, hid, ((0,), (0,))).astype(BF16)
        pair[i].start()
    for i in range(heads):
        q[i] = acc[0, :, i * head_size:(i + 1) * head_size].astype(BF16)

    cross = []
    for i in range(heads):
        pair[i].wait_recv()
        half[i] = (grad[i, own_half].astype(F32) + pair_in[i].astype(F32)).astype(BF16)
        for k in range(1, chips):
            to = lax.rem(chip + k, chips)
            cross.append(ar_copy(1 + k, i, half.at[(i,) + cut(to)], chip_in.at[i, k], (to * 2 + core, h)))
            cross[-1].start()
    back_to = []
    mine = cut(chip, core * half_rows)
    for i in range(heads):
        total = half[(i,) + cut(chip)].astype(F32)
        for k in range(1, chips):
            cross[i * (chips - 1) + k - 1].wait_recv()
            total = total + chip_in[i, k].astype(F32)
        grad_sum[(i,) + mine] = total.astype(BF16)
        for k in range(1, chips):
            to = lax.rem(chip + k, chips)
            spot = grad_sum.at[(i,) + mine]
            back_to.append(ar_copy(chips + k, i, spot, spot, (to * 2 + core, h)))
            back_to[-1].start()

    def attend(i):
        chunk = 128
        keys_n = WINDOW + chunk
        for b in range(rows // chunk):
            first = b * chunk
            keys = kv[i, first:first + keys_n]
            scores = dot(q[i, first:first + chunk], keys, ((1,), (1,))) * head_size ** (-0.5)
            r = lax.broadcasted_iota(jnp.int32, scores.shape, 0)
            c = lax.broadcasted_iota(jnp.int32, scores.shape, 1)
            allowed = (c > r) & (c <= r + WINDOW) & (c >= WINDOW - first - t * rows)
            scores = jnp.where(allowed, scores, -1e30)
            top = jnp.max(scores, axis=-1, keepdims=True)
            expo = jnp.exp(scores - top)
            weights = (expo * (1.0 / jnp.sum(expo, axis=-1, keepdims=True))).astype(BF16)
            att[i, first:first + chunk] = dot(weights, kv[heads + i, first:first + keys_n])

    for p, spot in order:
        ag_copy(p, spot).wait_send()
    for c in pair + cross:
        c.wait_send()
    for c in halo:
        c.wait()
    for i in range(heads):
        attend(i)
    last = []
    for i in range(heads):
        for k in range(1, chips):
            back_to[i * (chips - 1) + k - 1].wait_recv()
        spot = grad_sum.at[i, own_half]
        last.append(ar_copy(2 * chips, i, spot, spot, other))
        last[-1].start()

    for c in back_to:
        c.wait_send()
    for i in range(heads):
        last[i].wait()

        def renew(j, matrix, fan_in):
            g = grad_sum[i, :, j * hidden:(j + 1) * hidden].astype(F32)
            mean_sq = jnp.sum(jnp.sum(g * g, axis=1, keepdims=True), axis=0, keepdims=True) / (head_size * hidden)
            return (matrix - (step[i] * fan_in ** (-0.5)) * g * lax.rsqrt(mean_sq + 1e-06)).astype(BF16)

        gw = renew(0, g_w[i], head_size)
        uw = renew(1, u_w[i], head_size)
        dw = renew(2, d_w[i].T, hidden)
        qn = unit(q[i].astype(F32)).astype(BF16)
        gate_pre = dot(qn, gw)
        hid = (gate_pre * jax.nn.sigmoid(gate_pre) * dot(qn, uw)).astype(BF16)
        fast = dot(hid, dw, ((1,), (1,)))
        comb[:, i * head_size:(i + 1) * head_size] = (att[i] + fast).astype(BF16)

    loads[7].wait()
    out_rows = out.shape[0]
    piece_cols = out.shape[1] // len(trees)

    def rs_copy(p, spot):
        axis, sign = trees[p][spot]
        k = p * 16 + slot(spot)
        return pltpu.make_async_remote_copy(
            src_ref=go_out.at[k], dst_ref=come_in.at[k], send_sem=rs_send.at[k], recv_sem=rs_recv.at[k],
            device_id=at((axis, -sign)), device_id_type=MESH,
        )

    def gathered(p, spot):
        own = part[p, pl.ds(pl.multiple_of(owner(spot) * out_rows, out_rows), out_rows)]
        for child in belows[p].get(spot, []):
            rs_copy(p, child).wait_recv()
            own = own + come_in[p * 16 + slot(child)].astype(F32)
        return own.astype(BF16)

    def fill(p):
        def cols(j, carry):
            lanes = pl.ds(pl.multiple_of(j * 256, 256), 256)
            wide = pl.ds(pl.multiple_of(p * piece_cols + j * 256, 256), 256)
            part[p, :, lanes] = dot(comb[...], w_o[:, wide])
            return carry

        lax.fori_loop(0, piece_cols // 256, cols, 0)

    filled, sent = 0, []
    for now, p, spot in plan_back(trees, out_rows * piece_cols * 2, times):
        while filled < len(trees) and (filled <= p or now >= PART * (filled + 1)):
            fill(filled)
            filled += 1
        go_out[p * 16 + slot(spot)] = gathered(p, spot)
        sent.append(rs_copy(p, spot))
        sent[-1].start()
        if len(sent) > LAG:
            sent[-1 - LAG].wait_send()
    for p in range(len(trees)):
        out[:, p * piece_cols:(p + 1) * piece_cols] = gathered(p, (0, 0))

    for c in sent[-LAG:]:
        c.wait_send()


def shards(
    tok_n, head_n, tokens, w_query, w_key, w_value, w_out, fast_gate, fast_up, fast_down, token_rate, head_step
):
    rows, width = tokens.shape
    depth, local_width = w_query.shape
    d_model = w_out.shape[1]
    heads, head_size, hidden = fast_gate.shape
    pieces = len(MIRRORS)
    any_space = pl.BlockSpec(memory_space=pl.ANY)
    vmem = pl.BlockSpec(memory_space=pltpu.VMEM)
    smem = pl.BlockSpec(memory_space=pltpu.SMEM)
    dma = pltpu.SemaphoreType.DMA
    return pl.pallas_call(
        functools.partial(kernel, tok_n),
        out_shape=jax.ShapeDtypeStruct((rows // head_n, d_model), BF16),
        in_specs=[any_space] * 8 + [vmem, smem],
        out_specs=vmem,
        scratch_shapes=[
            pltpu.VMEM((head_n, rows, width), BF16),
            pltpu.VMEM((3, depth, local_width), BF16),
            pltpu.VMEM((local_width, d_model), BF16),
            pltpu.VMEM((3, rows, local_width), F32),
            pltpu.VMEM((heads, rows, head_size), BF16),
            pltpu.VMEM((2 * heads, WINDOW + rows, head_size), BF16),
            pltpu.VMEM((heads, head_size, hidden), F32),
            pltpu.VMEM((heads, head_size, hidden), F32),
            pltpu.VMEM((heads, hidden, head_size), F32),
            pltpu.VMEM((heads, head_size, 3 * hidden), BF16),
            pltpu.VMEM((heads, head_size // 2, 3 * hidden), BF16),
            pltpu.VMEM((heads, head_size // 2, 3 * hidden), BF16),
            pltpu.VMEM((heads, tok_n // 2, 2 * head_size // tok_n, 3 * hidden // 2), BF16),
            pltpu.VMEM((heads, head_size, 3 * hidden), BF16),
            pltpu.VMEM((heads, rows, head_size), F32),
            pltpu.VMEM((rows, local_width), BF16),
            pltpu.VMEM((pieces, rows, d_model // pieces), F32),
            pltpu.VMEM((pieces * 16, rows // head_n, d_model // pieces), BF16),
            pltpu.VMEM((pieces * 16, rows // head_n, d_model // pieces), BF16),
            dma((8,)), dma((pieces * 16,)), dma((pieces * 16,)), dma((2 * heads,)), dma((2 * heads,)),
            dma(((tok_n + 1) * heads,)), dma(((tok_n + 1) * heads,)), dma((pieces * 16,)), dma((pieces * 16,)),
        ],
        compiler_params=pltpu.CompilerParams(
            collective_id=0, has_side_effects=True, vmem_limit_bytes=60 * 2**20
        ),
    )(tokens, w_query, w_key, w_value, w_out, fast_gate, fast_up, fast_down, token_rate.T, head_step)


def solution(mesh):
    placed = (
        P("tok", "head"),
        P(None, "head"),
        P(None, "head"),
        P(None, "head"),
        P("head", None),
        P("head", None, None),
        P("head", None, None),
        P("head", None, None),
        P("tok", "head"),
        P("head"),
    )
    return jax.shard_map(
        functools.partial(shards, mesh.shape["tok"], mesh.shape["head"]),
        mesh=mesh, in_specs=placed, out_specs=P(("tok", "head"), None), check_vma=False,
    )
```

```python
import functools
import heapq

import jax
import jax.numpy as jnp
from jax import lax
from jax.experimental import pallas as pl
from jax.experimental.pallas import tpu as pltpu
from jax.sharding import PartitionSpec as P

MESH = pl.DeviceIdType.MESH
WINDOW = 512
SIDE = 4
RX, RZ, LX, LZ = 43.5e3, 21.7e3, 1.8, 3.5
AHEAD = 2.0
PART = 1.2
LATE = 4.0
UNIT = 0.25
AG_SEMS, RS_SEMS = 51, 32
F32 = jnp.float32
BF16 = jnp.bfloat16
MIRRORS = ((1, 1), (-1, 1), (1, -1), (-1, -1))


def tree_of(sx, sz):
    come = {(0, sz % 4): ("z", sz), (0, -sz % 4): ("z", -sz)}
    for b in (0, 1, 3):
        come[(sx % 4, b)] = ("x", sx)
        come[(-sx % 4, b)] = ("x", -sx)
        come[(2, b)] = ("x", sx)
    come[(0, 2)] = ("z", sz)
    come[(-sx % 4, 2)] = ("x", -sx)
    come[(sx % 4, 2)] = ("z", -sz)
    come[(2, 2)] = ("z", sz)
    return come


def from_of(spot, way):
    axis, sign = way
    return ((spot[0] - sign) % 4, spot[1]) if axis == "x" else (spot[0], (spot[1] - sign) % 4)


def below_of(come):
    below = {}
    for spot, way in come.items():
        below.setdefault(from_of(spot, way), []).append(spot)
    return below


def height(below, spot):
    return max([1 + height(below, s) for s in below.get(spot, [])], default=0)


def plan(trees, size):
    rate = {"x": RX, "z": RZ}
    late = {"x": LX, "z": LZ}
    belows = [below_of(t) for t in trees]
    queue = {(a, s): [] for a in "xz" for s in (1, -1)}
    free = dict.fromkeys(queue, 0.0)
    heap, count, done = [], 0, []

    def add(piece, spot):
        nonlocal count
        for to in belows[piece].get(spot, []):
            count += 1
            rank = -height(belows[piece], to)
            heapq.heappush(queue[trees[piece][to]], (rank, count, piece, to))

    def run(now):
        nonlocal count
        for way, waiting in queue.items():
            if waiting and free[way] <= now:
                _, _, piece, to = heapq.heappop(waiting)
                free[way] = now + size / rate[way[0]]
                count += 1
                heapq.heappush(heap, (free[way], count, None))
                count += 1
                heapq.heappush(heap, (free[way] + late[way[0]], count, (now, piece, to)))

    for piece in range(len(trees)):
        add(piece, (0, 0))
    run(0.0)
    while heap:
        now, _, got = heapq.heappop(heap)
        if got:
            done.append((got[0], now, got[1], got[2]))
            add(got[1], got[2])
        run(now)
    return done


def plan_back(trees, size, times):
    rate = {"x": RX, "z": RZ}
    late = {"x": LX, "z": LZ}
    belows = [below_of(t) for t in trees]
    rank = {(p, spot): -end for _, end, p, spot in times}
    left = {(p, spot): len(belows[p].get(spot, [])) + 1 for p, spot in rank}
    queue = {(a, s): [] for a in "xz" for s in (1, -1)}
    free = dict.fromkeys(queue, 0.0)
    heap = [(PART * (p + 1), p, (p, spot)) for p, spot in rank]
    heapq.heapify(heap)
    count, order = len(trees), []
    while heap:
        now, _, got = heapq.heappop(heap)
        if got and got[1] != (0, 0):
            left[got] -= 1
            if left[got] == 0:
                heapq.heappush(queue[trees[got[0]][got[1]]], (rank[got], got))
        if heap and heap[0][0] == now:
            continue
        for way, waiting in queue.items():
            if waiting and free[way] <= now:
                _, (p, spot) = heapq.heappop(waiting)
                free[way] = now + size / rate[way[0]]
                order.append((now, p, spot))
                count += 1
                heapq.heappush(heap, (free[way], count, None))
                count += 1
                heapq.heappush(heap, (free[way] + late[way[0]], count, (p, from_of(spot, trees[p][spot]))))
    return order


def slot(spot):
    return spot[0] * SIDE + spot[1]


def dot(a, b, dims=((1,), (0,))):
    return lax.dot_general(a, b, (dims, ((), ())), preferred_element_type=F32)


def unit(u):
    return u * lax.rsqrt(jnp.mean(u * u, axis=-1, keepdims=True) + 1e-06)


def kernel(
    tok_n, tokens, w_query, w_key, w_value, w_out, gate, upper, down, rate, step,
    out,
    blocks, w_in, w_o, acc, q, kv, g_w, u_w, d_w,
    grad, pair_in, half, chip_in, grad_sum, att, comb, part, come_in, go_out,
    load_sem, ag_send, ag_recv, halo_sem, ar_send, ar_recv, rs_send, rs_recv,
):
    rows = tokens.shape[0]
    width = tokens.shape[1]
    heads, head_size, hidden = g_w.shape
    t = lax.axis_index("tok")
    h = lax.axis_index("head")
    x, z = h // SIDE, lax.rem(h, SIDE)

    def at_(way):
        axis, sign = way
        if axis == "x":
            return (t, lax.rem(x + (SIDE + sign), SIDE) * SIDE + z)
        return (t, x * SIDE + lax.rem(z + (SIDE + sign), SIDE))

    nbr = {(a, s): at_((a, s)) for a in "xz" for s in (1, -1)}

    def at(way):
        return nbr[way]

    def owner(spot):
        a, b = spot
        return lax.rem(x + (SIDE - a), SIDE) * SIDE + lax.rem(z + (SIDE - b), SIDE)

    def tok_at(k):
        return (lax.rem(t + k, tok_n), h)

    def drain(ref, sem):
        pltpu.make_async_copy(ref, ref, sem).wait()

    loads = [pltpu.make_async_copy(tokens, blocks.at[0], load_sem.at[0])]
    for j, w in enumerate((w_query, w_key, w_value)):
        loads.append(pltpu.make_async_copy(w, w_in.at[j], load_sem.at[1]))
    loads.append(pltpu.make_async_copy(gate, g_w, load_sem.at[2]))
    loads.append(pltpu.make_async_copy(upper, u_w, load_sem.at[3]))
    loads.append(pltpu.make_async_copy(down, d_w, load_sem.at[4]))
    loads.append(pltpu.make_async_copy(w_out, w_o, load_sem.at[5]))
    for c in loads:
        c.start()

    barrier = pltpu.get_barrier_semaphore()
    ways = [("x", 1), ("x", -1), ("z", 1), ("z", -1)]
    for way in ways:
        pl.semaphore_signal(barrier, inc=1, device_id=at(way), device_id_type=MESH)
    near = [1, tok_n - 1] + list(range(2, tok_n, 2))
    for k in near:
        pl.semaphore_signal(barrier, inc=1, device_id=tok_at(k), device_id_type=MESH)
    pl.semaphore_wait(barrier, len(ways) + len(near))

    trees = [tree_of(*m) for m in MIRRORS]
    belows = [below_of(tr) for tr in trees]
    piece_rows = rows // len(trees)
    times = plan(trees, piece_rows * width * 2)
    order = [(p, spot) for _, _, p, spot in times]
    script = [(end, 0, p, spot) for _, end, p, spot in times]
    came = {(p, spot): end for _, end, p, spot in times}
    for begin, _, p, spot in times:
        frm = from_of(spot, trees[p][spot])
        script.append((max(begin - AHEAD, came.get((p, frm), -1.0)), 1, p, spot))
    script.sort(key=lambda e: e[:2])

    finish = {}
    for p, spot in order:
        finish[spot] = max(finish.get(spot, 0.0), came[p, spot])
    late = [spot for spot in finish if finish[spot] > max(finish.values()) - LATE]
    shared, seat = {}, {}
    for p, spot in order:
        if spot not in late and spot not in belows[p]:
            shared.setdefault(spot, []).append(p)
    for p, spot in order:
        key = spot if p in shared.get(spot, []) else (p, spot)
        seat[p, spot] = seat.setdefault(key, len(set(seat.values())))

    def ag_copy(p, to):
        frm = from_of(to, trees[p][to])
        span = pl.ds(p * piece_rows, piece_rows)
        src = tokens.at[span] if frm == (0, 0) else blocks.at[slot(frm), span]
        return pltpu.make_async_remote_copy(
            src_ref=src, dst_ref=blocks.at[slot(to), span], send_sem=ag_send.at[0], recv_sem=ag_recv.at[seat[p, to]],
            device_id=at(trees[p][to]), device_id_type=MESH,
        )

    early = [e for e in script if e[1] == 1 and e[0] <= 0.0]
    script = [e for e in script if not (e[1] == 1 and e[0] <= 0.0)]
    for _, _, p, spot in early:
        ag_copy(p, spot).start()

    def project(spot, span, low, high, first=False):
        base = pl.multiple_of(owner(spot) * width, width)

        def one(j, carry):
            prod = dot(blocks[slot(spot), span], w_in[j, pl.ds(base, width)])
            acc[j, span] = prod if first else acc[j, span] + prod
            return carry

        if high == low + 1:
            one(low, 0)
        else:
            lax.fori_loop(low, high, one, 0)

    every = slice(0, rows)
    loads[0].wait()
    drain(w_in, load_sem.at[1])
    project((0, 0), every, 0, 3, True)
    missing = dict.fromkeys(finish, len(trees))
    work, later, clock = [], [], 0.0
    for n, (now, sends, p, spot) in enumerate(script):
        clock = max(clock, now)
        if sends:
            ag_copy(p, spot).start()
        else:
            missing[spot] -= 1
            group = shared.get(spot, [])
            if p not in group:
                ag_copy(p, spot).wait_recv()
            elif came[p, spot] == max(came[g, spot] for g in group) and p == max(
                g for g in group if came[g, spot] == came[p, spot]
            ):
                drain(blocks.at[slot(spot), pl.ds(0, len(group) * piece_rows)], ag_recv.at[seat[p, spot]])
            if spot in late:
                work.append((spot, slice(p * piece_rows, (p + 1) * piece_rows), 1))
                work.append((spot, slice(p * piece_rows, (p + 1) * piece_rows), 2))
                if missing[spot] == 0:
                    later.append((spot, every, 0))
            elif missing[spot] == 0:
                work.append((spot, every, 1))
                work.append((spot, every, 2))
                later.append((spot, every, 0))
        until = script[n + 1][0] if n + 1 < len(script) else clock
        while (work or later) and clock + UNIT / 2 <= until:
            where, span, j = (work or later).pop(0)
            project(where, span, j, j + 1)
            clock += UNIT if span is every else UNIT / 2
    for where, span, j in work:
        project(where, span, j, j + 1)

    for i in range(heads):
        cols = slice(i * head_size, (i + 1) * head_size)
        kv[i, pl.ds(WINDOW, rows)] = acc[1, :, cols].astype(BF16)
        kv[heads + i, pl.ds(WINDOW, rows)] = acc[2, :, cols].astype(BF16)
    for i in range(2 * heads):
        pltpu.make_async_remote_copy(
            src_ref=kv.at[i, pl.ds(rows, WINDOW)], dst_ref=kv.at[i, pl.ds(0, WINDOW)],
            send_sem=halo_sem.at[0], recv_sem=halo_sem.at[1], device_id=tok_at(1), device_id_type=MESH,
        ).start()

    for c in loads[4:7]:
        c.wait()
    core = lax.rem(t, 2)
    chip = t // 2
    chips = tok_n // 2
    other = (t + 1 - 2 * core, h)
    half_rows = head_size // 2
    own_half = pl.ds(pl.multiple_of(core * half_rows, half_rows), half_rows)
    other_half = pl.ds(pl.multiple_of((1 - core) * half_rows, half_rows), half_rows)
    cut_rows, cut_cols = 2 * half_rows // chips, 3 * hidden // 2

    def cut(s, base=0):
        return (
            pl.ds(pl.multiple_of(base + (s // 2) * cut_rows, cut_rows), cut_rows),
            pl.ds(pl.multiple_of(lax.rem(s, 2) * cut_cols, cut_cols), cut_cols),
        )

    def column(row):
        n = row.shape[1]
        wide = jnp.broadcast_to(row, (n, n))
        eye = lax.broadcasted_iota(jnp.int32, (n, n), 0) == lax.broadcasted_iota(jnp.int32, (n, n), 1)
        return jnp.sum(jnp.where(eye, wide, 0.0), axis=1, keepdims=True)

    def ar_copy(kind, i, src, dst, to):
        return pltpu.make_async_remote_copy(
            src_ref=src, dst_ref=dst, send_sem=ar_send.at[kind], recv_sem=ar_recv.at[kind * heads + i],
            device_id=to, device_id_type=MESH,
        )

    pair = [ar_copy(0, i, grad.at[i, other_half], pair_in.at[i], other) for i in range(heads)]
    here = pl.ds(WINDOW, rows)
    for i in range(heads):
        gw = g_w[i].astype(BF16)
        uw = u_w[i].astype(BF16)
        dw = d_w[i].astype(BF16)
        kn = unit(kv[i, here].astype(F32)).astype(BF16)
        each = jnp.concatenate([column(rate[i:i + 1, r:r + 128]) for r in range(0, rows, 128)], axis=0)
        tg = (-each * kv[heads + i, here].astype(F32)).astype(BF16)
        gate_pre = dot(kn, gw)
        up_pre = dot(kn, uw)
        back = dot(tg, dw, ((1,), (1,)))
        sigma = jax.nn.sigmoid(gate_pre)
        active = gate_pre * sigma
        hid = (active * up_pre).astype(BF16)
        d_up = (back * active).astype(BF16)
        d_gate = (back * up_pre * sigma * (1.0 + gate_pre * (1.0 - sigma))).astype(BF16)
        grad[i, :, 0:hidden] = dot(kn, d_gate, ((0,), (0,))).astype(BF16)
        grad[i, :, hidden:2 * hidden] = dot(kn, d_up, ((0,), (0,))).astype(BF16)
        grad[i, :, 2 * hidden:] = dot(tg, hid, ((0,), (0,))).astype(BF16)
        pair[i].start()
    for where, span, j in later:
        project(where, span, j, j + 1)
    for i in range(heads):
        q[i] = acc[0, :, i * head_size:(i + 1) * head_size].astype(BF16)

    for i in range(heads):
        pair[i].wait_recv()
        half[i] = (grad[i, own_half].astype(F32) + pair_in[i].astype(F32)).astype(BF16)
        for k in range(1, chips):
            to = lax.rem(chip + k, chips)
            ar_copy(1, i, half.at[(i,) + cut(to)], chip_in.at[i, k], (to * 2 + core, h)).start()
    mine = cut(chip, core * half_rows)
    for i in range(heads):
        total = half[(i,) + cut(chip)].astype(F32)
        drain(chip_in.at[i, pl.ds(1, chips - 1)], ar_recv.at[heads + i])
        for k in range(1, chips):
            total = total + chip_in[i, k].astype(F32)
        grad_sum[(i,) + mine] = total.astype(BF16)
        for k in range(1, chips):
            to = lax.rem(chip + k, chips)
            spot = grad_sum.at[(i,) + mine]
            ar_copy(2, i, spot, spot, (to * 2 + core, h)).start()

    def attend(i):
        chunk = 128
        keys_n = WINDOW + chunk
        for b in range(rows // chunk):
            first = b * chunk
            keys = kv[i, first:first + keys_n]
            scores = dot(q[i, first:first + chunk], keys, ((1,), (1,))) * head_size ** (-0.5)
            r = lax.broadcasted_iota(jnp.int32, scores.shape, 0)
            c = lax.broadcasted_iota(jnp.int32, scores.shape, 1)
            allowed = (c > r) & (c <= r + WINDOW) & (c >= WINDOW - first - t * rows)
            scores = jnp.where(allowed, scores, -1e30)
            top = jnp.max(scores, axis=-1, keepdims=True)
            expo = jnp.exp(scores - top)
            weights = (expo * (1.0 / jnp.sum(expo, axis=-1, keepdims=True))).astype(BF16)
            att[i, first:first + chunk] = dot(weights, kv[heads + i, first:first + keys_n])

    drain(kv.at[:, pl.ds(0, WINDOW)], halo_sem.at[1])
    for i in range(heads):
        attend(i)
    last = []
    for i in range(heads):
        drain(chip_in.at[i, pl.ds(1, chips - 1)], ar_recv.at[2 * heads + i])
        spot = grad_sum.at[i, own_half]
        last.append(ar_copy(3, i, spot, spot, other))
        last[-1].start()

    for i in range(heads):
        last[i].wait_recv()

        def renew(j, matrix, fan_in):
            g = grad_sum[i, :, j * hidden:(j + 1) * hidden].astype(F32)
            mean_sq = jnp.sum(jnp.sum(g * g, axis=1, keepdims=True), axis=0, keepdims=True) / (head_size * hidden)
            return (matrix - (step[i] * fan_in ** (-0.5)) * g * lax.rsqrt(mean_sq + 1e-06)).astype(BF16)

        gw = renew(0, g_w[i], head_size)
        uw = renew(1, u_w[i], head_size)
        dw = renew(2, d_w[i].T, hidden)
        qn = unit(q[i].astype(F32)).astype(BF16)
        gate_pre = dot(qn, gw)
        hid = (gate_pre * jax.nn.sigmoid(gate_pre) * dot(qn, uw)).astype(BF16)
        fast = dot(hid, dw, ((1,), (1,)))
        comb[:, i * head_size:(i + 1) * head_size] = (att[i] + fast).astype(BF16)

    loads[7].wait()
    out_rows = out.shape[0]
    piece_cols = out.shape[1] // len(trees)

    node = {}
    for p in range(len(trees)):
        for spot in belows[p]:
            node[p, spot] = len(node)

    def rs_copy(p, spot):
        axis, sign = trees[p][spot]
        frm = from_of(spot, trees[p][spot])
        k = seats[p, frm] + belows[p][frm].index(spot)
        return pltpu.make_async_remote_copy(
            src_ref=go_out.at[p * 16 + slot(spot)], dst_ref=come_in.at[k],
            send_sem=rs_send.at[0], recv_sem=rs_recv.at[node[p, frm]],
            device_id=at((axis, -sign)), device_id_type=MESH,
        )

    seats, taken = {}, 0
    for p, spot in node:
        seats[p, spot] = taken
        taken += len(belows[p][spot])

    def gathered(p, spot):
        own = part[p, pl.ds(pl.multiple_of(owner(spot) * out_rows, out_rows), out_rows)]
        n = len(belows[p].get(spot, []))
        if n:
            drain(come_in.at[pl.ds(seats[p, spot], n)], rs_recv.at[node[p, spot]])
            for k in range(n):
                own = own + come_in[seats[p, spot] + k].astype(F32)
        return own.astype(BF16)

    def fill(p):
        def cols(j, carry):
            lanes = pl.ds(pl.multiple_of(j * 256, 256), 256)
            wide = pl.ds(pl.multiple_of(p * piece_cols + j * 256, 256), 256)
            part[p, :, lanes] = dot(comb[...], w_o[:, wide])
            return carry

        lax.fori_loop(0, piece_cols // 256, cols, 0)

    filled = 0
    for now, p, spot in plan_back(trees, out_rows * piece_cols * 2, times):
        while filled < len(trees) and (filled <= p or now >= PART * (filled + 1)):
            fill(filled)
            filled += 1
        go_out[p * 16 + slot(spot)] = gathered(p, spot)
        rs_copy(p, spot).start()
    for p in range(len(trees)):
        out[:, p * piece_cols:(p + 1) * piece_cols] = gathered(p, (0, 0))

    drain(blocks.at[pl.ds(0, blocks.shape[0] - 1)], ag_send.at[0])
    drain(kv.at[:, pl.ds(0, WINDOW)], halo_sem.at[0])
    for kind, ref in enumerate((pair_in, chip_in.at[:, pl.ds(1, chips - 1)], chip_in.at[:, pl.ds(1, chips - 1)], pair_in)):
        drain(ref, ar_send.at[kind])
    drain(come_in.at[pl.ds(0, taken)], rs_send.at[0])


def shards(
    tok_n, head_n, tokens, w_query, w_key, w_value, w_out, fast_gate, fast_up, fast_down, token_rate, head_step
):
    rows, width = tokens.shape
    depth, local_width = w_query.shape
    d_model = w_out.shape[1]
    heads, head_size, hidden = fast_gate.shape
    pieces = len(MIRRORS)
    any_space = pl.BlockSpec(memory_space=pl.ANY)
    vmem = pl.BlockSpec(memory_space=pltpu.VMEM)
    smem = pl.BlockSpec(memory_space=pltpu.SMEM)
    dma = pltpu.SemaphoreType.DMA
    return pl.pallas_call(
        functools.partial(kernel, tok_n),
        out_shape=jax.ShapeDtypeStruct((rows // head_n, d_model), BF16),
        in_specs=[any_space] * 8 + [vmem, smem],
        out_specs=vmem,
        scratch_shapes=[
            pltpu.VMEM((head_n, rows, width), BF16),
            pltpu.VMEM((3, depth, local_width), BF16),
            pltpu.VMEM((local_width, d_model), BF16),
            pltpu.VMEM((3, rows, local_width), F32),
            pltpu.VMEM((heads, rows, head_size), BF16),
            pltpu.VMEM((2 * heads, WINDOW + rows, head_size), BF16),
            pltpu.VMEM((heads, head_size, hidden), F32),
            pltpu.VMEM((heads, head_size, hidden), F32),
            pltpu.VMEM((heads, hidden, head_size), F32),
            pltpu.VMEM((heads, head_size, 3 * hidden), BF16),
            pltpu.VMEM((heads, head_size // 2, 3 * hidden), BF16),
            pltpu.VMEM((heads, head_size // 2, 3 * hidden), BF16),
            pltpu.VMEM((heads, tok_n // 2, 2 * head_size // tok_n, 3 * hidden // 2), BF16),
            pltpu.VMEM((heads, head_size, 3 * hidden), BF16),
            pltpu.VMEM((heads, rows, head_size), F32),
            pltpu.VMEM((rows, local_width), BF16),
            pltpu.VMEM((pieces, rows, d_model // pieces), F32),
            pltpu.VMEM((pieces * 16, rows // head_n, d_model // pieces), BF16),
            pltpu.VMEM((pieces * 16, rows // head_n, d_model // pieces), BF16),
            dma((6,)), dma((1,)), dma((AG_SEMS,)), dma((2,)),
            dma((4,)), dma((4 * heads,)), dma((1,)), dma((RS_SEMS,)),
        ],
        compiler_params=pltpu.CompilerParams(
            collective_id=0, has_side_effects=True, vmem_limit_bytes=60 * 2**20
        ),
    )(tokens, w_query, w_key, w_value, w_out, fast_gate, fast_up, fast_down, token_rate.T, head_step)


def solution(mesh):
    placed = (
        P("tok", "head"),
        P(None, "head"),
        P(None, "head"),
        P(None, "head"),
        P("head", None),
        P("head", None, None),
        P("head", None, None),
        P("head", None, None),
        P("tok", "head"),
        P("head"),
    )
    return jax.shard_map(
        functools.partial(shards, mesh.shape["tok"], mesh.shape["head"]),
        mesh=mesh, in_specs=placed, out_specs=P(("tok", "head"), None), check_vma=False,
    )
```

```python
import functools
import heapq

import jax
import jax.numpy as jnp
from jax import lax
from jax.experimental import pallas as pl
from jax.experimental.pallas import tpu as pltpu
from jax.sharding import PartitionSpec as P

MESH = pl.DeviceIdType.MESH
WINDOW = 512
SIDE = 4
RX, RZ, LX, LZ = 43.5e3, 21.7e3, 1.8, 3.5
AHEAD = 2.0
PART = 1.2
LATE = 4.0
UNIT = 0.25
AG_SEMS, RS_SEMS = 51, 32
F32 = jnp.float32
BF16 = jnp.bfloat16
MIRRORS = ((1, 1), (-1, 1), (1, -1), (-1, -1))


def tree_of(sx, sz):
    come = {(0, sz % 4): ("z", sz), (0, -sz % 4): ("z", -sz)}
    for b in (0, 1, 3):
        come[(sx % 4, b)] = ("x", sx)
        come[(-sx % 4, b)] = ("x", -sx)
        come[(2, b)] = ("x", sx)
    come[(0, 2)] = ("z", sz)
    come[(-sx % 4, 2)] = ("x", -sx)
    come[(sx % 4, 2)] = ("z", -sz)
    come[(2, 2)] = ("z", sz)
    return come


def from_of(spot, way):
    axis, sign = way
    return ((spot[0] - sign) % 4, spot[1]) if axis == "x" else (spot[0], (spot[1] - sign) % 4)


def below_of(come):
    below = {}
    for spot, way in come.items():
        below.setdefault(from_of(spot, way), []).append(spot)
    return below


def height(below, spot):
    return max([1 + height(below, s) for s in below.get(spot, [])], default=0)


def plan(trees, size):
    rate = {"x": RX, "z": RZ}
    late = {"x": LX, "z": LZ}
    belows = [below_of(t) for t in trees]
    queue = {(a, s): [] for a in "xz" for s in (1, -1)}
    free = dict.fromkeys(queue, 0.0)
    heap, count, done = [], 0, []

    def add(piece, spot):
        nonlocal count
        for to in belows[piece].get(spot, []):
            count += 1
            rank = -height(belows[piece], to)
            heapq.heappush(queue[trees[piece][to]], (rank, count, piece, to))

    def run(now):
        nonlocal count
        for way, waiting in queue.items():
            if waiting and free[way] <= now:
                _, _, piece, to = heapq.heappop(waiting)
                free[way] = now + size / rate[way[0]]
                count += 1
                heapq.heappush(heap, (free[way], count, None))
                count += 1
                heapq.heappush(heap, (free[way] + late[way[0]], count, (now, piece, to)))

    for piece in range(len(trees)):
        add(piece, (0, 0))
    run(0.0)
    while heap:
        now, _, got = heapq.heappop(heap)
        if got:
            done.append((got[0], now, got[1], got[2]))
            add(got[1], got[2])
        run(now)
    return done


def plan_back(trees, size, times):
    rate = {"x": RX, "z": RZ}
    late = {"x": LX, "z": LZ}
    belows = [below_of(t) for t in trees]
    rank = {(p, spot): -end for _, end, p, spot in times}
    left = {(p, spot): len(belows[p].get(spot, [])) + 1 for p, spot in rank}
    queue = {(a, s): [] for a in "xz" for s in (1, -1)}
    free = dict.fromkeys(queue, 0.0)
    heap = [(PART * (p + 1), p, (p, spot)) for p, spot in rank]
    heapq.heapify(heap)
    count, order = len(trees), []
    while heap:
        now, _, got = heapq.heappop(heap)
        if got and got[1] != (0, 0):
            left[got] -= 1
            if left[got] == 0:
                heapq.heappush(queue[trees[got[0]][got[1]]], (rank[got], got))
        if heap and heap[0][0] == now:
            continue
        for way, waiting in queue.items():
            if waiting and free[way] <= now:
                _, (p, spot) = heapq.heappop(waiting)
                free[way] = now + size / rate[way[0]]
                order.append((now, p, spot))
                count += 1
                heapq.heappush(heap, (free[way], count, None))
                count += 1
                heapq.heappush(heap, (free[way] + late[way[0]], count, (p, from_of(spot, trees[p][spot]))))
    return order


def slot(spot):
    return spot[0] * SIDE + spot[1]


def dot(a, b, dims=((1,), (0,))):
    return lax.dot_general(a, b, (dims, ((), ())), preferred_element_type=F32)


def unit(u):
    return u * lax.rsqrt(jnp.mean(u * u, axis=-1, keepdims=True) + 1e-06)


def kernel(
    tok_n, tokens, w_query, w_key, w_value, w_out, gate, upper, down, rate_in, step_in,
    out,
    blocks, w_in, w_o, acc, q, kv, g_w, u_w, d_w, rate, step,
    grad, pair_in, half, chip_in, grad_sum, att, comb, part, come_in, go_out,
    load_sem, ag_send, ag_recv, halo_sem, ar_send, ar_recv, rs_send, rs_recv,
):
    rows = tokens.shape[0]
    width = tokens.shape[1]
    heads, head_size, hidden = g_w.shape
    t = lax.axis_index("tok")
    h = lax.axis_index("head")
    x, z = h // SIDE, lax.rem(h, SIDE)

    def at_(way):
        axis, sign = way
        if axis == "x":
            return (t, lax.rem(x + (SIDE + sign), SIDE) * SIDE + z)
        return (t, x * SIDE + lax.rem(z + (SIDE + sign), SIDE))

    nbr = {(a, s): at_((a, s)) for a in "xz" for s in (1, -1)}

    def at(way):
        return nbr[way]

    def owner(spot):
        a, b = spot
        return lax.rem(x + (SIDE - a), SIDE) * SIDE + lax.rem(z + (SIDE - b), SIDE)

    def tok_at(k):
        return (lax.rem(t + k, tok_n), h)

    def drain(ref, sem):
        pltpu.make_async_copy(ref, ref, sem).wait()

    loads = [pltpu.make_async_copy(tokens, blocks.at[0], load_sem.at[0])]
    for j, w in enumerate((w_query, w_key, w_value)):
        loads.append(pltpu.make_async_copy(w, w_in.at[j], load_sem.at[1]))
    loads.append(pltpu.make_async_copy(gate, g_w, load_sem.at[2]))
    loads.append(pltpu.make_async_copy(upper, u_w, load_sem.at[3]))
    loads.append(pltpu.make_async_copy(down, d_w, load_sem.at[4]))
    loads.append(pltpu.make_async_copy(rate_in, rate, load_sem.at[6]))
    loads.append(pltpu.make_async_copy(step_in, step, load_sem.at[7]))
    loads.append(pltpu.make_async_copy(w_out, w_o, load_sem.at[5]))
    for c in loads:
        c.start()

    barrier = pltpu.get_barrier_semaphore()
    ways = [("x", 1), ("x", -1), ("z", 1), ("z", -1)]
    for way in ways:
        pl.semaphore_signal(barrier, inc=1, device_id=at(way), device_id_type=MESH)
    near = [1, tok_n - 1] + list(range(2, tok_n, 2))
    for k in near:
        pl.semaphore_signal(barrier, inc=1, device_id=tok_at(k), device_id_type=MESH)
    pl.semaphore_wait(barrier, len(ways) + len(near))

    trees = [tree_of(*m) for m in MIRRORS]
    belows = [below_of(tr) for tr in trees]
    piece_rows = rows // len(trees)
    times = plan(trees, piece_rows * width * 2)
    order = [(p, spot) for _, _, p, spot in times]
    script = [(end, 0, p, spot) for _, end, p, spot in times]
    came = {(p, spot): end for _, end, p, spot in times}
    for begin, _, p, spot in times:
        frm = from_of(spot, trees[p][spot])
        script.append((max(begin - AHEAD, came.get((p, frm), -1.0)), 1, p, spot))
    script.sort(key=lambda e: e[:2])

    finish = {}
    for p, spot in order:
        finish[spot] = max(finish.get(spot, 0.0), came[p, spot])
    late = [spot for spot in finish if finish[spot] > max(finish.values()) - LATE]
    shared, seat = {}, {}
    for p, spot in order:
        if spot not in late and spot not in belows[p]:
            shared.setdefault(spot, []).append(p)
    for p, spot in order:
        key = spot if p in shared.get(spot, []) else (p, spot)
        seat[p, spot] = seat.setdefault(key, len(set(seat.values())))

    def ag_copy(p, to):
        frm = from_of(to, trees[p][to])
        span = pl.ds(p * piece_rows, piece_rows)
        src = tokens.at[span] if frm == (0, 0) else blocks.at[slot(frm), span]
        return pltpu.make_async_remote_copy(
            src_ref=src, dst_ref=blocks.at[slot(to), span], send_sem=ag_send.at[0], recv_sem=ag_recv.at[seat[p, to]],
            device_id=at(trees[p][to]), device_id_type=MESH,
        )

    early = [e for e in script if e[1] == 1 and e[0] <= 0.0]
    script = [e for e in script if not (e[1] == 1 and e[0] <= 0.0)]
    for _, _, p, spot in early:
        ag_copy(p, spot).start()

    def project(spot, span, low, high, first=False):
        base = pl.multiple_of(owner(spot) * width, width)

        def one(j, carry):
            prod = dot(blocks[slot(spot), span], w_in[j, pl.ds(base, width)])
            acc[j, span] = prod if first else acc[j, span] + prod
            return carry

        if high == low + 1:
            one(low, 0)
        else:
            lax.fori_loop(low, high, one, 0)

    every = slice(0, rows)
    loads[0].wait()
    drain(w_in, load_sem.at[1])
    project((0, 0), every, 0, 3, True)
    missing = dict.fromkeys(finish, len(trees))
    work, later, clock = [], [], 0.0
    for n, (now, sends, p, spot) in enumerate(script):
        clock = max(clock, now)
        if sends:
            ag_copy(p, spot).start()
        else:
            missing[spot] -= 1
            group = shared.get(spot, [])
            if p not in group:
                ag_copy(p, spot).wait_recv()
            elif came[p, spot] == max(came[g, spot] for g in group) and p == max(
                g for g in group if came[g, spot] == came[p, spot]
            ):
                drain(blocks.at[slot(spot), pl.ds(0, len(group) * piece_rows)], ag_recv.at[seat[p, spot]])
            if spot in late:
                work.append((spot, slice(p * piece_rows, (p + 1) * piece_rows), 1))
                work.append((spot, slice(p * piece_rows, (p + 1) * piece_rows), 2))
                if missing[spot] == 0:
                    later.append((spot, every, 0))
            elif missing[spot] == 0:
                work.append((spot, every, 1))
                work.append((spot, every, 2))
                later.append((spot, every, 0))
        until = script[n + 1][0] if n + 1 < len(script) else clock
        while (work or later) and clock + UNIT / 2 <= until:
            where, span, j = (work or later).pop(0)
            project(where, span, j, j + 1)
            clock += UNIT if span is every else UNIT / 2
    for where, span, j in work:
        project(where, span, j, j + 1)

    for i in range(heads):
        cols = slice(i * head_size, (i + 1) * head_size)
        kv[i, pl.ds(WINDOW, rows)] = acc[1, :, cols].astype(BF16)
        kv[heads + i, pl.ds(WINDOW, rows)] = acc[2, :, cols].astype(BF16)
    for i in range(2 * heads):
        pltpu.make_async_remote_copy(
            src_ref=kv.at[i, pl.ds(rows, WINDOW)], dst_ref=kv.at[i, pl.ds(0, WINDOW)],
            send_sem=halo_sem.at[0], recv_sem=halo_sem.at[1], device_id=tok_at(1), device_id_type=MESH,
        ).start()

    for c in loads[4:9]:
        c.wait()
    core = lax.rem(t, 2)
    chip = t // 2
    chips = tok_n // 2
    other = (t + 1 - 2 * core, h)
    half_rows = head_size // 2
    own_half = pl.ds(pl.multiple_of(core * half_rows, half_rows), half_rows)
    other_half = pl.ds(pl.multiple_of((1 - core) * half_rows, half_rows), half_rows)
    cut_rows, cut_cols = 2 * half_rows // chips, 3 * hidden // 2

    def cut(s, base=0):
        return (
            pl.ds(pl.multiple_of(base + (s // 2) * cut_rows, cut_rows), cut_rows),
            pl.ds(pl.multiple_of(lax.rem(s, 2) * cut_cols, cut_cols), cut_cols),
        )

    def column(row):
        n = row.shape[1]
        wide = jnp.broadcast_to(row, (n, n))
        eye = lax.broadcasted_iota(jnp.int32, (n, n), 0) == lax.broadcasted_iota(jnp.int32, (n, n), 1)
        return jnp.sum(jnp.where(eye, wide, 0.0), axis=1, keepdims=True)

    def ar_copy(kind, i, src, dst, to):
        return pltpu.make_async_remote_copy(
            src_ref=src, dst_ref=dst, send_sem=ar_send.at[kind], recv_sem=ar_recv.at[kind * heads + i],
            device_id=to, device_id_type=MESH,
        )

    pair = [ar_copy(0, i, grad.at[i, other_half], pair_in.at[i], other) for i in range(heads)]
    here = pl.ds(WINDOW, rows)
    for i in range(heads):
        gw = g_w[i].astype(BF16)
        uw = u_w[i].astype(BF16)
        dw = d_w[i].astype(BF16)
        kn = unit(kv[i, here].astype(F32)).astype(BF16)
        each = jnp.concatenate([column(rate[i:i + 1, r:r + 128]) for r in range(0, rows, 128)], axis=0)
        tg = (-each * kv[heads + i, here].astype(F32)).astype(BF16)
        gate_pre = dot(kn, gw)
        up_pre = dot(kn, uw)
        back = dot(tg, dw, ((1,), (1,)))
        sigma = jax.nn.sigmoid(gate_pre)
        active = gate_pre * sigma
        hid = (active * up_pre).astype(BF16)
        d_up = (back * active).astype(BF16)
        d_gate = (back * up_pre * sigma * (1.0 + gate_pre * (1.0 - sigma))).astype(BF16)
        grad[i, :, 0:hidden] = dot(kn, d_gate, ((0,), (0,))).astype(BF16)
        grad[i, :, hidden:2 * hidden] = dot(kn, d_up, ((0,), (0,))).astype(BF16)
        grad[i, :, 2 * hidden:] = dot(tg, hid, ((0,), (0,))).astype(BF16)
        pair[i].start()

    for i in range(heads):
        pair[i].wait_recv()
        half[i] = (grad[i, own_half].astype(F32) + pair_in[i].astype(F32)).astype(BF16)
        for k in range(1, chips):
            to = lax.rem(chip + k, chips)
            ar_copy(1, i, half.at[(i,) + cut(to)], chip_in.at[i, k], (to * 2 + core, h)).start()
    for where, span, j in later:
        project(where, span, j, j + 1)
    for i in range(heads):
        q[i] = acc[0, :, i * head_size:(i + 1) * head_size].astype(BF16)
    mine = cut(chip, core * half_rows)
    for i in range(heads):
        total = half[(i,) + cut(chip)].astype(F32)
        drain(chip_in.at[i, pl.ds(1, chips - 1)], ar_recv.at[heads + i])
        for k in range(1, chips):
            total = total + chip_in[i, k].astype(F32)
        grad_sum[(i,) + mine] = total.astype(BF16)
        for k in range(1, chips):
            to = lax.rem(chip + k, chips)
            spot = grad_sum.at[(i,) + mine]
            ar_copy(2, i, spot, spot, (to * 2 + core, h)).start()

    def attend(i):
        chunk = 128
        keys_n = WINDOW + chunk
        for b in range(rows // chunk):
            first = b * chunk
            keys = kv[i, first:first + keys_n]
            scores = dot(q[i, first:first + chunk], keys, ((1,), (1,))) * head_size ** (-0.5)
            r = lax.broadcasted_iota(jnp.int32, scores.shape, 0)
            c = lax.broadcasted_iota(jnp.int32, scores.shape, 1)
            allowed = (c > r) & (c <= r + WINDOW) & (c >= WINDOW - first - t * rows)
            scores = jnp.where(allowed, scores, -1e30)
            top = jnp.max(scores, axis=-1, keepdims=True)
            expo = jnp.exp(scores - top)
            weights = (expo * (1.0 / jnp.sum(expo, axis=-1, keepdims=True))).astype(BF16)
            att[i, first:first + chunk] = dot(weights, kv[heads + i, first:first + keys_n])

    drain(kv.at[:, pl.ds(0, WINDOW)], halo_sem.at[1])
    for i in range(heads):
        attend(i)
    last = []
    for i in range(heads):
        drain(chip_in.at[i, pl.ds(1, chips - 1)], ar_recv.at[2 * heads + i])
        spot = grad_sum.at[i, own_half]
        last.append(ar_copy(3, i, spot, spot, other))
        last[-1].start()

    for i in range(heads):
        last[i].wait_recv()

        def renew(j, matrix, fan_in):
            g = grad_sum[i, :, j * hidden:(j + 1) * hidden].astype(F32)
            mean_sq = jnp.sum(jnp.sum(g * g, axis=1, keepdims=True), axis=0, keepdims=True) / (head_size * hidden)
            return (matrix - (step[i] * fan_in ** (-0.5)) * g * lax.rsqrt(mean_sq + 1e-06)).astype(BF16)

        gw = renew(0, g_w[i], head_size)
        uw = renew(1, u_w[i], head_size)
        dw = renew(2, d_w[i].T, hidden)
        qn = unit(q[i].astype(F32)).astype(BF16)
        gate_pre = dot(qn, gw)
        hid = (gate_pre * jax.nn.sigmoid(gate_pre) * dot(qn, uw)).astype(BF16)
        fast = dot(hid, dw, ((1,), (1,)))
        comb[:, i * head_size:(i + 1) * head_size] = (att[i] + fast).astype(BF16)

    loads[9].wait()
    out_rows = out.shape[0]
    piece_cols = out.shape[1] // len(trees)

    node = {}
    for p in range(len(trees)):
        for spot in belows[p]:
            node[p, spot] = len(node)

    def rs_copy(p, spot):
        axis, sign = trees[p][spot]
        frm = from_of(spot, trees[p][spot])
        k = seats[p, frm] + belows[p][frm].index(spot)
        return pltpu.make_async_remote_copy(
            src_ref=go_out.at[p * 16 + slot(spot)], dst_ref=come_in.at[k],
            send_sem=rs_send.at[0], recv_sem=rs_recv.at[node[p, frm]],
            device_id=at((axis, -sign)), device_id_type=MESH,
        )

    seats, taken = {}, 0
    for p, spot in node:
        seats[p, spot] = taken
        taken += len(belows[p][spot])

    def gathered(p, spot):
        own = part[p, pl.ds(pl.multiple_of(owner(spot) * out_rows, out_rows), out_rows)]
        n = len(belows[p].get(spot, []))
        if n:
            drain(come_in.at[pl.ds(seats[p, spot], n)], rs_recv.at[node[p, spot]])
            for k in range(n):
                own = own + come_in[seats[p, spot] + k].astype(F32)
        return own.astype(BF16)

    def fill(p):
        def cols(j, carry):
            lanes = pl.ds(pl.multiple_of(j * 256, 256), 256)
            wide = pl.ds(pl.multiple_of(p * piece_cols + j * 256, 256), 256)
            part[p, :, lanes] = dot(comb[...], w_o[:, wide])
            return carry

        lax.fori_loop(0, piece_cols // 256, cols, 0)

    filled = 0
    for now, p, spot in plan_back(trees, out_rows * piece_cols * 2, times):
        while filled < len(trees) and (filled <= p or now >= PART * (filled + 1)):
            fill(filled)
            filled += 1
        go_out[p * 16 + slot(spot)] = gathered(p, spot)
        rs_copy(p, spot).start()
    for p in range(len(trees)):
        out[:, p * piece_cols:(p + 1) * piece_cols] = gathered(p, (0, 0))

    drain(blocks.at[pl.ds(0, blocks.shape[0] - 1)], ag_send.at[0])
    drain(kv.at[:, pl.ds(0, WINDOW)], halo_sem.at[0])
    for kind, ref in enumerate((pair_in, chip_in.at[:, pl.ds(1, chips - 1)], chip_in.at[:, pl.ds(1, chips - 1)], pair_in)):
        drain(ref, ar_send.at[kind])
    drain(come_in.at[pl.ds(0, taken)], rs_send.at[0])


def shards(
    tok_n, head_n, tokens, w_query, w_key, w_value, w_out, fast_gate, fast_up, fast_down, token_rate, head_step
):
    rows, width = tokens.shape
    depth, local_width = w_query.shape
    d_model = w_out.shape[1]
    heads, head_size, hidden = fast_gate.shape
    pieces = len(MIRRORS)
    any_space = pl.BlockSpec(memory_space=pl.ANY)
    vmem = pl.BlockSpec(memory_space=pltpu.VMEM)
    dma = pltpu.SemaphoreType.DMA
    return pl.pallas_call(
        functools.partial(kernel, tok_n),
        out_shape=jax.ShapeDtypeStruct((rows // head_n, d_model), BF16),
        in_specs=[any_space] * 10,
        out_specs=vmem,
        scratch_shapes=[
            pltpu.VMEM((head_n, rows, width), BF16),
            pltpu.VMEM((3, depth, local_width), BF16),
            pltpu.VMEM((local_width, d_model), BF16),
            pltpu.VMEM((3, rows, local_width), F32),
            pltpu.VMEM((heads, rows, head_size), BF16),
            pltpu.VMEM((2 * heads, WINDOW + rows, head_size), BF16),
            pltpu.VMEM((heads, head_size, hidden), F32),
            pltpu.VMEM((heads, head_size, hidden), F32),
            pltpu.VMEM((heads, hidden, head_size), F32),
            pltpu.VMEM((heads, rows), F32),
            pltpu.SMEM((heads,), F32),
            pltpu.VMEM((heads, head_size, 3 * hidden), BF16),
            pltpu.VMEM((heads, head_size // 2, 3 * hidden), BF16),
            pltpu.VMEM((heads, head_size // 2, 3 * hidden), BF16),
            pltpu.VMEM((heads, tok_n // 2, 2 * head_size // tok_n, 3 * hidden // 2), BF16),
            pltpu.VMEM((heads, head_size, 3 * hidden), BF16),
            pltpu.VMEM((heads, rows, head_size), F32),
            pltpu.VMEM((rows, local_width), BF16),
            pltpu.VMEM((pieces, rows, d_model // pieces), F32),
            pltpu.VMEM((pieces * 16, rows // head_n, d_model // pieces), BF16),
            pltpu.VMEM((pieces * 16, rows // head_n, d_model // pieces), BF16),
            dma((8,)), dma((1,)), dma((AG_SEMS,)), dma((2,)),
            dma((4,)), dma((4 * heads,)), dma((1,)), dma((RS_SEMS,)),
        ],
        compiler_params=pltpu.CompilerParams(
            collective_id=0, has_side_effects=True, vmem_limit_bytes=60 * 2**20
        ),
    )(tokens, w_query, w_key, w_value, w_out, fast_gate, fast_up, fast_down, token_rate.T, head_step)


def solution(mesh):
    placed = (
        P("tok", "head"),
        P(None, "head"),
        P(None, "head"),
        P(None, "head"),
        P("head", None),
        P("head", None, None),
        P("head", None, None),
        P("head", None, None),
        P("tok", "head"),
        P("head"),
    )
    return jax.shard_map(
        functools.partial(shards, mesh.shape["tok"], mesh.shape["head"]),
        mesh=mesh, in_specs=placed, out_specs=P(("tok", "head"), None), check_vma=False,
    )
```

```python
import functools
import heapq

import jax
import jax.numpy as jnp
from jax import lax
from jax.experimental import pallas as pl
from jax.experimental.pallas import tpu as pltpu
from jax.sharding import PartitionSpec as P

MESH = pl.DeviceIdType.MESH
WINDOW = 512
SIDE = 4
RX, RZ, LX, LZ = 43.5e3, 21.7e3, 1.8, 3.5
AHEAD = 2.0
PART = 1.5
LATE = 4.0
UNIT = 0.25
AG_SEMS, RS_SEMS = 51, 32
F32 = jnp.float32
BF16 = jnp.bfloat16
MIRRORS = ((1, 1), (-1, 1), (1, -1), (-1, -1))


def tree_of(sx, sz):
    come = {(0, sz % 4): ("z", sz), (0, -sz % 4): ("z", -sz)}
    for b in (0, 1, 3):
        come[(sx % 4, b)] = ("x", sx)
        come[(-sx % 4, b)] = ("x", -sx)
        come[(2, b)] = ("x", sx)
    come[(0, 2)] = ("z", sz)
    come[(-sx % 4, 2)] = ("x", -sx)
    come[(sx % 4, 2)] = ("z", -sz)
    come[(2, 2)] = ("z", sz)
    return come


def from_of(spot, way):
    axis, sign = way
    return ((spot[0] - sign) % 4, spot[1]) if axis == "x" else (spot[0], (spot[1] - sign) % 4)


def below_of(come):
    below = {}
    for spot, way in come.items():
        below.setdefault(from_of(spot, way), []).append(spot)
    return below


def height(below, spot):
    return max([1 + height(below, s) for s in below.get(spot, [])], default=0)


def plan(trees, size):
    rate = {"x": RX, "z": RZ}
    late = {"x": LX, "z": LZ}
    belows = [below_of(t) for t in trees]
    queue = {(a, s): [] for a in "xz" for s in (1, -1)}
    free = dict.fromkeys(queue, 0.0)
    heap, count, done = [], 0, []

    def add(piece, spot):
        nonlocal count
        for to in belows[piece].get(spot, []):
            count += 1
            rank = -height(belows[piece], to)
            heapq.heappush(queue[trees[piece][to]], (rank, count, piece, to))

    def run(now):
        nonlocal count
        for way, waiting in queue.items():
            if waiting and free[way] <= now:
                _, _, piece, to = heapq.heappop(waiting)
                free[way] = now + size / rate[way[0]]
                count += 1
                heapq.heappush(heap, (free[way], count, None))
                count += 1
                heapq.heappush(heap, (free[way] + late[way[0]], count, (now, piece, to)))

    for piece in range(len(trees)):
        add(piece, (0, 0))
    run(0.0)
    while heap:
        now, _, got = heapq.heappop(heap)
        if got:
            done.append((got[0], now, got[1], got[2]))
            add(got[1], got[2])
        run(now)
    return done


def plan_back(trees, size, times):
    rate = {"x": RX, "z": RZ}
    late = {"x": LX, "z": LZ}
    belows = [below_of(t) for t in trees]
    rank = {(p, spot): -end for _, end, p, spot in times}
    left = {(p, spot): len(belows[p].get(spot, [])) + 1 for p, spot in rank}
    queue = {(a, s): [] for a in "xz" for s in (1, -1)}
    free = dict.fromkeys(queue, 0.0)
    heap = [(PART * (p + 1), p, (p, spot)) for p, spot in rank]
    heapq.heapify(heap)
    count, order = len(trees), []
    while heap:
        now, _, got = heapq.heappop(heap)
        if got and got[1] != (0, 0):
            left[got] -= 1
            if left[got] == 0:
                heapq.heappush(queue[trees[got[0]][got[1]]], (rank[got], got))
        if heap and heap[0][0] == now:
            continue
        for way, waiting in queue.items():
            if waiting and free[way] <= now:
                _, (p, spot) = heapq.heappop(waiting)
                free[way] = now + size / rate[way[0]]
                order.append((now, p, spot))
                count += 1
                heapq.heappush(heap, (free[way], count, None))
                count += 1
                heapq.heappush(heap, (free[way] + late[way[0]], count, (p, from_of(spot, trees[p][spot]))))
    return order


def slot(spot):
    return spot[0] * SIDE + spot[1]


def dot(a, b, dims=((1,), (0,))):
    return lax.dot_general(a, b, (dims, ((), ())), preferred_element_type=F32)


def unit(u):
    return u * lax.rsqrt(jnp.mean(u * u, axis=-1, keepdims=True) + 1e-06)


def kernel(
    tok_n, tokens, w_query, w_key, w_value, w_out, gate, upper, down, rate_in, step_in,
    out,
    blocks, w_in, w_o, acc, q, kv, g_w, u_w, d_w, rate, step,
    grad, pair_in, half, chip_in, grad_sum, att, comb, part, come_in, go_out,
    load_sem, ag_send, ag_recv, halo_sem, ar_send, ar_recv, rs_send, rs_recv,
):
    rows = tokens.shape[0]
    width = tokens.shape[1]
    heads, head_size, hidden = g_w.shape
    t = lax.axis_index("tok")
    h = lax.axis_index("head")
    x, z = h // SIDE, lax.rem(h, SIDE)

    def at_(way):
        axis, sign = way
        if axis == "x":
            return (t, lax.rem(x + (SIDE + sign), SIDE) * SIDE + z)
        return (t, x * SIDE + lax.rem(z + (SIDE + sign), SIDE))

    nbr = {(a, s): at_((a, s)) for a in "xz" for s in (1, -1)}

    def at(way):
        return nbr[way]

    def owner(spot):
        a, b = spot
        return lax.rem(x + (SIDE - a), SIDE) * SIDE + lax.rem(z + (SIDE - b), SIDE)

    def tok_at(k):
        return (lax.rem(t + k, tok_n), h)

    def drain(ref, sem):
        pltpu.make_async_copy(ref, ref, sem).wait()

    loads = [pltpu.make_async_copy(tokens, blocks.at[0], load_sem.at[0])]
    for j, w in enumerate((w_query, w_key, w_value)):
        loads.append(pltpu.make_async_copy(w, w_in.at[j], load_sem.at[1]))
    loads.append(pltpu.make_async_copy(gate, g_w, load_sem.at[2]))
    loads.append(pltpu.make_async_copy(upper, u_w, load_sem.at[3]))
    loads.append(pltpu.make_async_copy(down, d_w, load_sem.at[4]))
    loads.append(pltpu.make_async_copy(rate_in, rate, load_sem.at[6]))
    loads.append(pltpu.make_async_copy(step_in, step, load_sem.at[7]))
    loads.append(pltpu.make_async_copy(w_out, w_o, load_sem.at[5]))
    for c in loads:
        c.start()

    barrier = pltpu.get_barrier_semaphore()
    ways = [("x", 1), ("x", -1), ("z", 1), ("z", -1)]
    for way in ways:
        pl.semaphore_signal(barrier, inc=1, device_id=at(way), device_id_type=MESH)
    near = [1, tok_n - 1] + list(range(2, tok_n, 2))
    for k in near:
        pl.semaphore_signal(barrier, inc=1, device_id=tok_at(k), device_id_type=MESH)
    pl.semaphore_wait(barrier, len(ways) + len(near))

    trees = [tree_of(*m) for m in MIRRORS]
    belows = [below_of(tr) for tr in trees]
    piece_rows = rows // len(trees)
    times = plan(trees, piece_rows * width * 2)
    order = [(p, spot) for _, _, p, spot in times]
    script = [(end, 0, p, spot) for _, end, p, spot in times]
    came = {(p, spot): end for _, end, p, spot in times}
    for begin, _, p, spot in times:
        frm = from_of(spot, trees[p][spot])
        script.append((max(begin - AHEAD, came.get((p, frm), -1.0)), 1, p, spot))
    script.sort(key=lambda e: e[:2])

    finish = {}
    for p, spot in order:
        finish[spot] = max(finish.get(spot, 0.0), came[p, spot])
    late = [spot for spot in finish if finish[spot] > max(finish.values()) - LATE]
    shared, seat = {}, {}
    for p, spot in order:
        if spot not in late and spot not in belows[p]:
            shared.setdefault(spot, []).append(p)
    for p, spot in order:
        key = spot if p in shared.get(spot, []) else (p, spot)
        seat[p, spot] = seat.setdefault(key, len(set(seat.values())))

    def ag_copy(p, to):
        frm = from_of(to, trees[p][to])
        span = pl.ds(p * piece_rows, piece_rows)
        src = tokens.at[span] if frm == (0, 0) else blocks.at[slot(frm), span]
        return pltpu.make_async_remote_copy(
            src_ref=src, dst_ref=blocks.at[slot(to), span], send_sem=ag_send.at[0], recv_sem=ag_recv.at[seat[p, to]],
            device_id=at(trees[p][to]), device_id_type=MESH,
        )

    early = [e for e in script if e[1] == 1 and e[0] <= 0.0]
    script = [e for e in script if not (e[1] == 1 and e[0] <= 0.0)]
    for _, _, p, spot in early:
        ag_copy(p, spot).start()

    def project(spot, span, low, high, first=False):
        base = pl.multiple_of(owner(spot) * width, width)

        def one(j, carry):
            prod = dot(blocks[slot(spot), span], w_in[j, pl.ds(base, width)])
            acc[j, span] = prod if first else acc[j, span] + prod
            return carry

        if high == low + 1:
            one(low, 0)
        else:
            lax.fori_loop(low, high, one, 0)

    every = slice(0, rows)
    loads[0].wait()
    drain(w_in, load_sem.at[1])
    project((0, 0), every, 0, 3, True)
    missing = dict.fromkeys(finish, len(trees))
    work, later, clock = [], [], 0.0
    for n, (now, sends, p, spot) in enumerate(script):
        clock = max(clock, now)
        if sends:
            ag_copy(p, spot).start()
        else:
            missing[spot] -= 1
            group = shared.get(spot, [])
            if p not in group:
                ag_copy(p, spot).wait_recv()
            elif came[p, spot] == max(came[g, spot] for g in group) and p == max(
                g for g in group if came[g, spot] == came[p, spot]
            ):
                drain(blocks.at[slot(spot), pl.ds(0, len(group) * piece_rows)], ag_recv.at[seat[p, spot]])
            if spot in late:
                work.append((spot, slice(p * piece_rows, (p + 1) * piece_rows), 1))
                work.append((spot, slice(p * piece_rows, (p + 1) * piece_rows), 2))
                if missing[spot] == 0:
                    later.append((spot, every, 0))
            elif missing[spot] == 0:
                work.append((spot, every, 1))
                work.append((spot, every, 2))
                later.append((spot, every, 0))
        until = script[n + 1][0] if n + 1 < len(script) else clock
        while (work or later) and clock + UNIT / 2 <= until:
            where, span, j = (work or later).pop(0)
            project(where, span, j, j + 1)
            clock += UNIT if span is every else UNIT / 2
    for where, span, j in work:
        project(where, span, j, j + 1)

    for i in range(heads):
        cols = slice(i * head_size, (i + 1) * head_size)
        kv[i, pl.ds(WINDOW, rows)] = acc[1, :, cols].astype(BF16)
        kv[heads + i, pl.ds(WINDOW, rows)] = acc[2, :, cols].astype(BF16)
    for i in range(2 * heads):
        pltpu.make_async_remote_copy(
            src_ref=kv.at[i, pl.ds(rows, WINDOW)], dst_ref=kv.at[i, pl.ds(0, WINDOW)],
            send_sem=halo_sem.at[0], recv_sem=halo_sem.at[1], device_id=tok_at(1), device_id_type=MESH,
        ).start()

    for c in loads[4:9]:
        c.wait()
    core = lax.rem(t, 2)
    chip = t // 2
    chips = tok_n // 2
    other = (t + 1 - 2 * core, h)
    half_rows = head_size // 2
    own_half = pl.ds(pl.multiple_of(core * half_rows, half_rows), half_rows)
    other_half = pl.ds(pl.multiple_of((1 - core) * half_rows, half_rows), half_rows)
    cut_rows, cut_cols = 2 * half_rows // chips, 3 * hidden // 2

    def cut(s, base=0):
        return (
            pl.ds(pl.multiple_of(base + (s // 2) * cut_rows, cut_rows), cut_rows),
            pl.ds(pl.multiple_of(lax.rem(s, 2) * cut_cols, cut_cols), cut_cols),
        )

    def column(row):
        n = row.shape[1]
        wide = jnp.broadcast_to(row, (n, n))
        eye = lax.broadcasted_iota(jnp.int32, (n, n), 0) == lax.broadcasted_iota(jnp.int32, (n, n), 1)
        return jnp.sum(jnp.where(eye, wide, 0.0), axis=1, keepdims=True)

    def ar_copy(kind, i, src, dst, to):
        return pltpu.make_async_remote_copy(
            src_ref=src, dst_ref=dst, send_sem=ar_send.at[kind], recv_sem=ar_recv.at[kind * heads + i],
            device_id=to, device_id_type=MESH,
        )

    pair = [ar_copy(0, i, grad.at[i, other_half], pair_in.at[i], other) for i in range(heads)]
    here = pl.ds(WINDOW, rows)
    for i in range(heads):
        gw = g_w[i].astype(BF16)
        uw = u_w[i].astype(BF16)
        dw = d_w[i].astype(BF16)
        kn = unit(kv[i, here].astype(F32)).astype(BF16)
        each = jnp.concatenate([column(rate[i:i + 1, r:r + 128]) for r in range(0, rows, 128)], axis=0)
        tg = (-each * kv[heads + i, here].astype(F32)).astype(BF16)
        gate_pre = dot(kn, gw)
        up_pre = dot(kn, uw)
        back = dot(tg, dw, ((1,), (1,)))
        sigma = jax.nn.sigmoid(gate_pre)
        active = gate_pre * sigma
        hid = (active * up_pre).astype(BF16)
        d_up = (back * active).astype(BF16)
        d_gate = (back * up_pre * sigma * (1.0 + gate_pre * (1.0 - sigma))).astype(BF16)
        grad[i, :, 0:hidden] = dot(kn, d_gate, ((0,), (0,))).astype(BF16)
        grad[i, :, hidden:2 * hidden] = dot(kn, d_up, ((0,), (0,))).astype(BF16)
        grad[i, :, 2 * hidden:] = dot(tg, hid, ((0,), (0,))).astype(BF16)
        pair[i].start()

    for i in range(heads):
        pair[i].wait_recv()
        half[i] = (grad[i, own_half].astype(F32) + pair_in[i].astype(F32)).astype(BF16)
        for k in range(1, chips):
            to = lax.rem(chip + k, chips)
            ar_copy(1, i, half.at[(i,) + cut(to)], chip_in.at[i, k], (to * 2 + core, h)).start()
    for where, span, j in later:
        project(where, span, j, j + 1)
    for i in range(heads):
        q[i] = acc[0, :, i * head_size:(i + 1) * head_size].astype(BF16)
    mine = cut(chip, core * half_rows)
    for i in range(heads):
        total = half[(i,) + cut(chip)].astype(F32)
        drain(chip_in.at[i, pl.ds(1, chips - 1)], ar_recv.at[heads + i])
        for k in range(1, chips):
            total = total + chip_in[i, k].astype(F32)
        grad_sum[(i,) + mine] = total.astype(BF16)
        for k in range(1, chips):
            to = lax.rem(chip + k, chips)
            spot = grad_sum.at[(i,) + mine]
            ar_copy(2, i, spot, spot, (to * 2 + core, h)).start()

    def attend(i):
        chunk = 128
        keys_n = WINDOW + chunk
        for b in range(rows // chunk):
            first = b * chunk
            keys = kv[i, first:first + keys_n]
            scores = dot(q[i, first:first + chunk], keys, ((1,), (1,))) * head_size ** (-0.5)
            r = lax.broadcasted_iota(jnp.int32, scores.shape, 0)
            c = lax.broadcasted_iota(jnp.int32, scores.shape, 1)
            allowed = (c > r) & (c <= r + WINDOW) & (c >= WINDOW - first - t * rows)
            scores = jnp.where(allowed, scores, -1e30)
            top = jnp.max(scores, axis=-1, keepdims=True)
            expo = jnp.exp(scores - top)
            weights = (expo * (1.0 / jnp.sum(expo, axis=-1, keepdims=True))).astype(BF16)
            att[i, first:first + chunk] = dot(weights, kv[heads + i, first:first + keys_n])

    drain(kv.at[:, pl.ds(0, WINDOW)], halo_sem.at[1])
    for i in range(heads):
        attend(i)
    last = []
    for i in range(heads):
        drain(chip_in.at[i, pl.ds(1, chips - 1)], ar_recv.at[2 * heads + i])
        spot = grad_sum.at[i, own_half]
        last.append(ar_copy(3, i, spot, spot, other))
        last[-1].start()

    for i in range(heads):
        last[i].wait_recv()

        def renew(j, matrix, fan_in):
            g = grad_sum[i, :, j * hidden:(j + 1) * hidden].astype(F32)
            mean_sq = jnp.sum(jnp.sum(g * g, axis=1, keepdims=True), axis=0, keepdims=True) / (head_size * hidden)
            return (matrix - (step[i] * fan_in ** (-0.5)) * g * lax.rsqrt(mean_sq + 1e-06)).astype(BF16)

        gw = renew(0, g_w[i], head_size)
        uw = renew(1, u_w[i], head_size)
        dw = renew(2, d_w[i].T, hidden)
        qn = unit(q[i].astype(F32)).astype(BF16)
        gate_pre = dot(qn, gw)
        hid = (gate_pre * jax.nn.sigmoid(gate_pre) * dot(qn, uw)).astype(BF16)
        fast = dot(hid, dw, ((1,), (1,)))
        comb[:, i * head_size:(i + 1) * head_size] = (att[i] + fast).astype(BF16)

    loads[9].wait()
    out_rows = out.shape[0]
    piece_cols = out.shape[1] // len(trees)

    node = {}
    for p in range(len(trees)):
        for spot in belows[p]:
            node[p, spot] = len(node)

    def rs_copy(p, spot):
        axis, sign = trees[p][spot]
        frm = from_of(spot, trees[p][spot])
        k = seats[p, frm] + belows[p][frm].index(spot)
        return pltpu.make_async_remote_copy(
            src_ref=go_out.at[p * 16 + slot(spot)], dst_ref=come_in.at[k],
            send_sem=rs_send.at[0], recv_sem=rs_recv.at[node[p, frm]],
            device_id=at((axis, -sign)), device_id_type=MESH,
        )

    seats, taken = {}, 0
    for p, spot in node:
        seats[p, spot] = taken
        taken += len(belows[p][spot])

    def gathered(p, spot):
        own = part[p, pl.ds(pl.multiple_of(owner(spot) * out_rows, out_rows), out_rows)]
        n = len(belows[p].get(spot, []))
        if n:
            drain(come_in.at[pl.ds(seats[p, spot], n)], rs_recv.at[node[p, spot]])
            for k in range(n):
                own = own + come_in[seats[p, spot] + k].astype(F32)
        return own.astype(BF16)

    def fill(p):
        def cols(j, carry):
            lanes = pl.ds(pl.multiple_of(j * 256, 256), 256)
            wide = pl.ds(pl.multiple_of(p * piece_cols + j * 256, 256), 256)
            part[p, :, lanes] = dot(comb[...], w_o[:, wide])
            return carry

        lax.fori_loop(0, piece_cols // 256, cols, 0)

    filled = 0
    for now, p, spot in plan_back(trees, out_rows * piece_cols * 2, times):
        while filled < len(trees) and (filled <= p or now >= PART * (filled + 1)):
            fill(filled)
            filled += 1
        go_out[p * 16 + slot(spot)] = gathered(p, spot)
        rs_copy(p, spot).start()
    for p in range(len(trees)):
        out[:, p * piece_cols:(p + 1) * piece_cols] = gathered(p, (0, 0))

    drain(blocks.at[pl.ds(0, blocks.shape[0] - 1)], ag_send.at[0])
    drain(kv.at[:, pl.ds(0, WINDOW)], halo_sem.at[0])
    for kind, ref in enumerate((pair_in, chip_in.at[:, pl.ds(1, chips - 1)], chip_in.at[:, pl.ds(1, chips - 1)], pair_in)):
        drain(ref, ar_send.at[kind])
    drain(come_in.at[pl.ds(0, taken)], rs_send.at[0])


def shards(
    tok_n, head_n, tokens, w_query, w_key, w_value, w_out, fast_gate, fast_up, fast_down, token_rate, head_step
):
    rows, width = tokens.shape
    depth, local_width = w_query.shape
    d_model = w_out.shape[1]
    heads, head_size, hidden = fast_gate.shape
    pieces = len(MIRRORS)
    any_space = pl.BlockSpec(memory_space=pl.ANY)
    vmem = pl.BlockSpec(memory_space=pltpu.VMEM)
    dma = pltpu.SemaphoreType.DMA
    return pl.pallas_call(
        functools.partial(kernel, tok_n),
        out_shape=jax.ShapeDtypeStruct((rows // head_n, d_model), BF16),
        in_specs=[any_space] * 10,
        out_specs=vmem,
        scratch_shapes=[
            pltpu.VMEM((head_n, rows, width), BF16),
            pltpu.VMEM((3, depth, local_width), BF16),
            pltpu.VMEM((local_width, d_model), BF16),
            pltpu.VMEM((3, rows, local_width), F32),
            pltpu.VMEM((heads, rows, head_size), BF16),
            pltpu.VMEM((2 * heads, WINDOW + rows, head_size), BF16),
            pltpu.VMEM((heads, head_size, hidden), F32),
            pltpu.VMEM((heads, head_size, hidden), F32),
            pltpu.VMEM((heads, hidden, head_size), F32),
            pltpu.VMEM((heads, rows), F32),
            pltpu.SMEM((heads,), F32),
            pltpu.VMEM((heads, head_size, 3 * hidden), BF16),
            pltpu.VMEM((heads, head_size // 2, 3 * hidden), BF16),
            pltpu.VMEM((heads, head_size // 2, 3 * hidden), BF16),
            pltpu.VMEM((heads, tok_n // 2, 2 * head_size // tok_n, 3 * hidden // 2), BF16),
            pltpu.VMEM((heads, head_size, 3 * hidden), BF16),
            pltpu.VMEM((heads, rows, head_size), F32),
            pltpu.VMEM((rows, local_width), BF16),
            pltpu.VMEM((pieces, rows, d_model // pieces), F32),
            pltpu.VMEM((pieces * 16, rows // head_n, d_model // pieces), BF16),
            pltpu.VMEM((pieces * 16, rows // head_n, d_model // pieces), BF16),
            dma((8,)), dma((1,)), dma((AG_SEMS,)), dma((2,)),
            dma((4,)), dma((4 * heads,)), dma((1,)), dma((RS_SEMS,)),
        ],
        compiler_params=pltpu.CompilerParams(
            collective_id=0, has_side_effects=True, vmem_limit_bytes=60 * 2**20
        ),
    )(tokens, w_query, w_key, w_value, w_out, fast_gate, fast_up, fast_down, token_rate.T, head_step)


def solution(mesh):
    placed = (
        P("tok", "head"),
        P(None, "head"),
        P(None, "head"),
        P(None, "head"),
        P("head", None),
        P("head", None, None),
        P("head", None, None),
        P("head", None, None),
        P("tok", "head"),
        P("head"),
    )
    return jax.shard_map(
        functools.partial(shards, mesh.shape["tok"], mesh.shape["head"]),
        mesh=mesh, in_specs=placed, out_specs=P(("tok", "head"), None), check_vma=False,
    )
```
